32 devices in a mesh: col: 16 (over z, y, x), row: 2 (over core).
Axes of the slice: x: 2, y: 2, z: 4, core: 2. Of those that a mesh axis runs over, the one named last changes fastest.
Arguments:
- rhs: bfloat16 [4, 16, 256, 512], P(None, 'col', 'row'), may hold values from -4 to 4
- leaf_rhs: bfloat16 [128, 256, 512], P(('col', 'row')), may hold values from -6 to 6
- leaf_inverse: bfloat16 [128, 256, 256], P(('col', 'row')), may hold values from -1 to 1.5
- leaf_lower: bfloat16 [4, 128, 256, 256], P(None, ('col', 'row')), may hold values from -0.0625 to 0.0625
- inverse_0: bfloat16 [4096, 256], P('col'), may hold values from -1 to 1.5
- inverse_1: bfloat16 [2048, 256], P('col'), may hold values from -1 to 1.5
- inverse_2: bfloat16 [1024, 256], P('col'), may hold values from -1 to 1.5
- inverse_3: bfloat16 [512, 256], P('col'), may hold values from -1 to 1.5
- lower_0: bfloat16 [3, 256, 4096], P(None, 'row', 'col'), may hold values from -0.1875 to 0.1875
- lower_1: bfloat16 [2, 256, 2048], P(None, 'row', 'col'), may hold values from -0.1875 to 0.1875
- lower_2: bfloat16 [1, 256, 1024], P(None, 'row', 'col'), may hold values from -0.1875 to 0.1875
- sparsity: int32 [6, 16, 8], P(None, 'col', 'row'), may hold values 0 or 1
Outputs:
- solution_0: bfloat16 [4096, 512], P('col')
- solution_1: bfloat16 [2048, 512], P('col')
- solution_2: bfloat16 [1024, 512], P('col')
- solution_3: bfloat16 [512, 512], P('col')
The draws below stay inside these ranges and needn't reach their ends.
All inputs are finite; a program needn't handle non-finite values. No bound on the sum of `sparsity` on one device may be relied on, other than what follows from the above.
Results may differ from the reference program's by a relative error of at most 0.015.
Values may be sent and summed in bfloat16 or wider, within the bound.
No kernel may reach another device: no remote copies, remote signals or barrier semaphores. Data moves between devices by JAX's collectives and lax.ppermute only.
A program may use at most 64 MiB of HBM per device.

```python
import math
import jax
import jax.numpy as jnp
from jax import lax

S = 256
K = 512
LEVELS = 4
NRB = 8
LEAVES_DEV = 4
LEAVES = 128
NODES_0 = 16
NODES_1 = 8
NODES_2 = 4
NODES_3 = 2
N_COL = 16
N_ROW = 2


def lower_triangle(key, count):
    key_diag, key_strict = jax.random.split(key)
    diagonal = jax.random.uniform(key_diag, (count, S), jnp.float32, 0.5, 1.5)
    strict = jnp.clip(jax.random.normal(key_strict, (count, S, S), jnp.float32), -6.0, 6.0) * (1.0 / math.sqrt(S))
    strict = jnp.clip(strict, -1.0, 1.0) * jnp.tril(jnp.ones((S, S), jnp.float32), -1)
    return strict + diagonal[:, :, None] * jnp.eye(S, dtype=jnp.float32)


def draw_leaf_inverse(key, part):
    return lower_triangle(jax.random.fold_in(key, 11), LEAVES).astype(jnp.bfloat16)


def draw_inverse_0(key, part):
    return lower_triangle(jax.random.fold_in(key, 20), NODES_0).reshape(NODES_0 * S, S).astype(jnp.bfloat16)


def draw_inverse_1(key, part):
    return lower_triangle(jax.random.fold_in(key, 21), NODES_1).reshape(NODES_1 * S, S).astype(jnp.bfloat16)


def draw_inverse_2(key, part):
    return lower_triangle(jax.random.fold_in(key, 22), NODES_2).reshape(NODES_2 * S, S).astype(jnp.bfloat16)


def draw_inverse_3(key, part):
    return lower_triangle(jax.random.fold_in(key, 23), NODES_3).reshape(NODES_3 * S, S).astype(jnp.bfloat16)


def with_ends(values, own_key, least, top_value):
    dims = values.shape
    index_at = [jax.random.randint(jax.random.fold_in(own_key, axis), (), 0, dims[axis]) for axis in range(len(dims))]
    values = values.at[tuple(index_at)].set(least)
    longest = dims.index(max(dims))
    index_at[longest] = (index_at[longest] + 1) % dims[longest]
    return values.at[tuple(index_at)].set(top_value)


def levels(key, shape, cuts, low, largest):
    gain = 1.0
    for position, blocks in cuts:
        steps = jax.random.uniform(jax.random.fold_in(jax.random.fold_in(key, 6), position), (blocks,), jnp.float32, low / len(cuts), largest / len(cuts))
        gain = gain * jnp.repeat(jnp.exp(steps), shape[position] // blocks).reshape((-1,) + (1,) * (len(shape) - 1 - position))
    return gain


def normal_values(rng, dims, width, reach, shards=(), held_as=jnp.bfloat16):
    drawn = width * jax.random.normal(rng, dims, jnp.float32)
    if shards:
        drawn = drawn * levels(rng, dims, shards, -0.22, 0.18)
    return jnp.clip(drawn, -reach, reach).astype(held_as)


def setup_inputs(seed: int = 0) -> dict:
    key_list = jax.random.split(jax.random.key(seed), 13)
    return {
        "rhs": normal_values(key_list[0], (LEVELS, N_COL, S, K), 0.5, 4.0, ((1, 16), (2, 2))),
        "leaf_rhs": normal_values(key_list[1], (LEAVES, S, K), 1.0, 6.0, ((0, 32),)),
        "leaf_inverse": draw_leaf_inverse(jax.random.fold_in(key_list[12], 71), 0),
        "leaf_lower": normal_values(key_list[3], (LEVELS, LEAVES, S, S), (S * LEAVES_DEV * N_ROW * 4) ** -0.5, 0.0625, ((1, 32),)),
        "inverse_0": draw_inverse_0(jax.random.fold_in(key_list[12], 71), 0),
        "inverse_1": draw_inverse_1(jax.random.fold_in(key_list[12], 71), 0),
        "inverse_2": draw_inverse_2(jax.random.fold_in(key_list[12], 71), 0),
        "inverse_3": draw_inverse_3(jax.random.fold_in(key_list[12], 71), 0),
        "lower_0": normal_values(key_list[8], (LEVELS - 1, S, NODES_0 * S), (4 * S) ** -0.5, 0.1875, ((1, 2), (2, 16))),
        "lower_1": normal_values(key_list[9], (LEVELS - 2, S, NODES_1 * S), (4 * S) ** -0.5, 0.1875, ((1, 2), (2, 16))),
        "lower_2": normal_values(key_list[10], (LEVELS - 3, S, NODES_2 * S), (4 * S) ** -0.5, 0.1875, ((1, 2), (2, 16))),
        "sparsity": with_ends((jax.random.randint(key_list[11], (6, N_COL, NRB), 0, 4) < 3).astype(jnp.int32), jax.random.fold_in(key_list[11], 1), 0, 1),
    }


def reference(rhs, leaf_rhs, leaf_inverse, leaf_lower, inverse_0, inverse_1, inverse_2, inverse_3, lower_0, lower_1, lower_2, sparsity):
    per_column = N_ROW * LEAVES_DEV

    def column_terms(column):
        first_leaf = (column * per_column).astype(jnp.int32)
        inverse_blocks = lax.dynamic_slice_in_dim(leaf_inverse, first_leaf, per_column, 0).astype(jnp.float32)
        right_sides = lax.dynamic_slice_in_dim(leaf_rhs, first_leaf, per_column, 0).astype(jnp.float32)
        leaf_solution = jnp.einsum("vrs,vsk->vrk", inverse_blocks, right_sides).astype(jnp.bfloat16)
        leaf_blocks = lax.dynamic_slice_in_dim(leaf_lower, first_leaf, per_column, 1).astype(jnp.float32)
        return jnp.einsum("mvrs,vsk->mrk", leaf_blocks, leaf_solution.astype(jnp.float32))

    leaf_update = lax.map(column_terms, jnp.arange(N_COL, dtype=jnp.int32))
    pending = []
    for height in range(LEVELS):
        group_size = 2 ** height
        assembled = rhs[height].astype(jnp.float32) - leaf_update[:, height]
        pending.append(assembled.reshape(N_COL // group_size, group_size, S, K).sum(axis=1))
    inverses = [inverse_0, inverse_1, inverse_2, inverse_3]
    lowers = [lower_0, lower_1, lower_2]
    bases = [0, 3, 5]
    outputs = []
    for height in range(LEVELS):
        node_count = N_COL // 2 ** height
        residual = pending[height].astype(jnp.bfloat16)
        inverse_blocks = inverses[height].reshape(node_count, S, S).astype(jnp.float32)
        solved = jnp.einsum("nrs,nsk->nrk", inverse_blocks, residual.astype(jnp.float32)).astype(jnp.bfloat16)
        outputs.append(solved.reshape(node_count * S, K))
        for ancestor in range(height + 1, LEVELS):
            pattern = sparsity[bases[height] + ancestor - height - 1]
            expanded = jnp.repeat(jnp.repeat(pattern, S // 2 ** height, axis=0), S // NRB, axis=1).T
            blocks = lowers[height][ancestor - height - 1].astype(jnp.float32) * expanded.astype(jnp.float32)
            update_sum = jnp.einsum("rnc,nck->nrk", blocks.reshape(S, node_count, S), solved.astype(jnp.float32))
            fan_ratio = 2 ** (ancestor - height)
            pending[ancestor] = pending[ancestor] - update_sum.reshape(node_count // fan_ratio, fan_ratio, S, K).sum(axis=1)
    return (outputs[0], outputs[1], outputs[2], outputs[3])
```

```python
import functools

import jax
import jax.numpy as jnp
from jax import lax
from jax.experimental import pallas as pl
from jax.experimental.pallas import tpu as pltpu
from jax.sharding import PartitionSpec as P

F32, BF16 = jnp.float32, jnp.bfloat16
WHOLE = pl.BlockSpec(memory_space=pltpu.VMEM)


def dot(a, b):
    return jnp.dot(a, b, preferred_element_type=F32)


def call(kernel, outs, *args, scratch=(), flops=0, name=None):
    outs = [jax.ShapeDtypeStruct(shape, dtype) for shape, dtype in outs]
    moved = sum(a.size * a.dtype.itemsize for a in (*args, *outs))
    single = len(outs) == 1
    return pl.pallas_call(
        kernel,
        out_shape=outs[0] if single else outs,
        in_specs=[WHOLE] * len(args),
        out_specs=WHOLE if single else [WHOLE] * len(outs),
        scratch_shapes=list(scratch),
        cost_estimate=pl.CostEstimate(flops=flops, bytes_accessed=moved, transcendentals=0),
        compiler_params=pltpu.CompilerParams(vmem_limit_bytes=16 << 20),
        name=name,
    )(*args)


def partner(block, axis, stride):
    count = lax.axis_size(axis)
    return lax.ppermute(block, axis, [(low, low ^ stride) for low in range(count)])


def halves(ref_like, half):
    me = lax.axis_index("row")
    return pl.ds(pl.multiple_of(me * half, half), half), pl.ds(
        pl.multiple_of((1 - me) * half, half), half
    )


def leaf_first(inverse, right, lower, top, solution_out, keep, send, total):
    leaves, size, _ = inverse.shape
    rows = top.shape[0]
    half = keep.shape[1]
    me = lax.axis_index("row")
    for v in range(leaves):
        solved = dot(inverse[v], right[v]).astype(BF16)
        solution_out[v] = solved
        term = dot(lower[v], solved)
        total[...] = -term if v == 0 else total[...] - term
    mine = pl.ds(pl.multiple_of(me * rows, rows), rows)
    total[mine, :] = total[mine, :] + top[...].astype(F32)
    own, other = halves(total, half)
    keep[...] = total[:, own]
    send[...] = total[:, other].astype(BF16)


def leaf_rest(solved, lower, top, keep, send, total):
    levels, leaves, size, _ = lower.shape
    rows = top.shape[1]
    half = keep.shape[2]
    me = lax.axis_index("row")
    mine = pl.ds(pl.multiple_of(me * rows, rows), rows)
    own, other = halves(total, half)
    for m in range(levels):
        acc = dot(lower[m, 0], solved[0])
        for v in range(1, leaves):
            acc = acc + dot(lower[m, v], solved[v])
        total[...] = -acc
        total[mine, :] = total[mine, :] + top[m].astype(F32)
        keep[m] = total[:, own]
        send[m] = total[:, other].astype(BF16)


def mask_lower(lower_0, lower_1, lower_2, pattern, out_0, out_1, out_2):
    rows = lower_0.shape[1]
    blocks = pattern.shape[2]
    spread = rows // blocks
    p = 0
    for lower, out in ((lower_0, out_0), (lower_1, out_1), (lower_2, out_2)):
        for m in range(lower.shape[0]):
            for b in range(blocks):
                at = pl.ds(b * spread, spread)
                factor = pattern[p, 0, b].astype(F32)
                out[m, at, :] = (lower[m, at, :].astype(F32) * factor).astype(BF16)
            p += 1


def by_core(own, other):
    first = lax.axis_index("row") == 0
    return jnp.where(first, own, other), jnp.where(first, other, own)


def level_zero(keep, got, inverse, low_own, low_other, keep_rest, got_rest, solved_out, p1, p2, p3):
    rows = low_own.shape[1]
    residual = (keep[...] + got[...].astype(F32)).astype(BF16)
    solved = dot(inverse[...], residual).astype(BF16)
    solved_out[...] = solved
    me = lax.axis_index("row")
    mine = pl.ds(pl.multiple_of(me * rows, rows), rows)
    theirs = pl.ds(pl.multiple_of((1 - me) * rows, rows), rows)
    for m, out in enumerate((p1, p2, p3)):
        for low, at in ((low_own, mine), (low_other, theirs)):
            total = keep_rest[m, at, :] + got_rest[m, at, :].astype(F32)
            out[at, :] = (total - dot(low[m], solved)).astype(out.dtype)


def level_one(own, got, inv_own, inv_x, low_oo, low_or, low_xo, low_xr, solved_out, u2, u3):
    part, size = inv_own.shape
    rows = low_oo.shape[1]
    residual = (own[...].astype(F32) + got[...].astype(F32)).astype(BF16)
    solved_own = dot(inv_own[...], residual).astype(BF16)
    solved_x = dot(inv_x[...], residual).astype(BF16)
    solved_out[...] = solved_own
    me = lax.axis_index("row")
    mine = pl.ds(pl.multiple_of(me * rows, rows), rows)
    theirs = pl.ds(pl.multiple_of((1 - me) * rows, rows), rows)
    for m, out in enumerate((u2, u3)):
        for low_a, low_b, at in ((low_oo, low_xo, mine), (low_or, low_xr, theirs)):
            out[at, :] = (dot(low_a[m], solved_own) + dot(low_b[m], solved_x)).astype(BF16)


def level_two(base, got, u_own, u_got, inv, low_own, low_other, rest, solved_out, v3):
    rows = low_own.shape[1]
    part = inv.shape[1]
    residual = (
        base[...].astype(F32) + got[...].astype(F32) - u_own[...].astype(F32) - u_got[...].astype(F32)
    ).astype(BF16)
    solved = [dot(inv[i], residual).astype(BF16) for i in range(inv.shape[0])]
    solved_out[...] = solved[0]
    me = lax.axis_index("row")
    mine = pl.ds(pl.multiple_of(me * rows, rows), rows)
    theirs = pl.ds(pl.multiple_of((1 - me) * rows, rows), rows)
    for low, at in ((low_own, mine), (low_other, theirs)):
        total = rest[at, :]
        for i in range(inv.shape[0]):
            total = total - dot(low[i], solved[i])
        v3[at, :] = total.astype(BF16)


def level_three(own, got, inverse, solved_out):
    residual = (own[...].astype(F32) + got[...].astype(F32)).astype(BF16)
    solved_out[...] = dot(inverse[...], residual).astype(BF16)


def join_halves(own, got, out):
    half = own.shape[1]
    mine, theirs = halves(out, half)
    out[:, mine] = own[...]
    out[:, theirs] = got[...]


def body(
    rhs, leaf_rhs, leaf_inverse, leaf_lower,
    inverse_0, inverse_1, inverse_2, inverse_3,
    lower_0, lower_1, lower_2, sparsity,
):
    levels, _, rows, width = rhs.shape
    leaves, size, _ = leaf_inverse.shape
    half = width // lax.axis_size("row")

    inv1_x = partner(inverse_1, "col", 1)
    inv2_x = partner(inverse_2, "col", 1)

    solved_leaf, keep0, send0 = call(
        leaf_first,
        [((leaves, size, width), BF16), ((size, half), F32), ((size, half), BF16)],
        leaf_inverse, leaf_rhs, leaf_lower[0], rhs[0, 0],
        scratch=[pltpu.VMEM((size, width), F32)],
        flops=4 * leaves * size * size * width, name="leaf_first",
    )
    low0, low1, low2 = pl.pallas_call(
        mask_lower,
        out_shape=[jax.ShapeDtypeStruct(x.shape, BF16) for x in (lower_0, lower_1, lower_2)],
        in_specs=[WHOLE] * 3 + [pl.BlockSpec(memory_space=pltpu.SMEM)],
        out_specs=[WHOLE] * 3,
        compiler_params=pltpu.CompilerParams(vmem_limit_bytes=16 << 20),
        name="mask_lower",
    )(lower_0, lower_1, lower_2, sparsity)
    low1_x = partner(low1, "col", 1)
    low2_x = partner(low2, "col", 1)
    low0_r = partner(low0, "row", 1)

    got0 = partner(send0, "row", 1)
    keep, send = call(
        leaf_rest,
        [((levels - 1, size, half), F32), ((levels - 1, size, half), BF16)],
        solved_leaf, leaf_lower[1:], rhs[1:, 0],
        scratch=[pltpu.VMEM((size, width), F32)],
        flops=2 * (levels - 1) * leaves * size * size * width, name="leaf_rest",
    )
    got = partner(send, "row", 1)
    sol0, p1, p2, p3 = call(
        level_zero,
        [((size, half), BF16)] * 4,
        keep0, got0, inverse_0, low0, low0_r, keep, got,
        flops=8 * size * size * half, name="level_zero",
    )
    p1_x = partner(p1, "col", 1)
    p2_y = partner(p2, "col", 2)
    p3_x = partner(p3, "col", 1)

    low1_r = partner(low1, "row", 1)
    low1_xr = partner(low1_x, "row", 1)
    inv2_y = partner(jnp.stack([inverse_2, inv2_x]), "col", 2)
    low2_y = partner(jnp.concatenate([low2, low2_x]), "col", 2)
    inv2 = jnp.concatenate([inverse_2[None], inv2_x[None], inv2_y])
    low2_all = jnp.concatenate([low2, low2_x, low2_y])
    low2_r = partner(low2_all, "row", 1)

    sol1, u2, u3 = call(
        level_one,
        [((inverse_1.shape[0], half), BF16)] + [((size, half), BF16)] * 2,
        p1, p1_x, inverse_1, inv1_x, low1, low1_r, low1_x, low1_xr,
        flops=6 * size * size * half, name="level_one",
    )
    u2_y = partner(u2, "col", 2)
    s2 = (p2.astype(F32) + p2_y.astype(F32)).astype(BF16)
    s2_x = partner(s2, "col", 1)
    s3 = (p3.astype(F32) + p3_x.astype(F32) - u3.astype(F32)).astype(BF16)
    s3_y = partner(s3, "col", 2)
    rest = s3.astype(F32) + s3_y.astype(F32)
    sol2, v3 = call(
        level_two,
        [((inverse_2.shape[0], half), BF16), ((size, half), BF16)],
        s2, s2_x, u2, u2_y, inv2, low2_all, low2_r, rest,
        flops=4 * size * size * half, name="level_two",
    )
    v3_z = partner(v3, "col", 4)
    sol3 = call(
        level_three,
        [((inverse_3.shape[0], half), BF16)],
        v3, v3_z, inverse_3, flops=2 * inverse_3.size * half, name="level_three",
    )
    outs = []
    for solved in (sol0, sol1, sol2, sol3):
        got_half = partner(solved, "row", 1)
        outs.append(call(join_halves, [((solved.shape[0], width), BF16)], solved, got_half, name="join"))
    return tuple(outs)


def solution(mesh):
    return jax.shard_map(
        body,
        mesh=mesh,
        in_specs=(
            P(None, "col", "row", None),
            P(("col", "row"), None, None),
            P(("col", "row"), None, None),
            P(None, ("col", "row"), None, None),
            P("col", None),
            P("col", None),
            P("col", None),
            P("col", None),
            P(None, "row", "col"),
            P(None, "row", "col"),
            P(None, "row", "col"),
            P(None, "col", "row"),
        ),
        out_specs=(P("col", None), P("col", None), P("col", None), P("col", None)),
        check_vma=False,
    )
```

```python
import jax
import jax.numpy as jnp
from jax import lax
from jax.experimental import pallas as pl
from jax.experimental.pallas import tpu as pltpu
from jax.sharding import PartitionSpec as P

F32, BF16 = jnp.float32, jnp.bfloat16
WHOLE = pl.BlockSpec(memory_space=pltpu.VMEM)
SCALARS = pl.BlockSpec(memory_space=pltpu.SMEM)


def dot(a, b):
    return jnp.dot(a, b, preferred_element_type=F32)


def dot_t(a, b):
    return lax.dot_general(a, b, (((0,), (0,)), ((), ())), preferred_element_type=F32)


def call(kernel, outs, *args, scratch=(), flops=0, specs=None):
    outs = [jax.ShapeDtypeStruct(shape, dtype) for shape, dtype in outs]
    moved = sum(a.size * a.dtype.itemsize for a in (*args, *outs))
    single = len(outs) == 1
    return pl.pallas_call(
        kernel,
        out_shape=outs[0] if single else outs,
        in_specs=specs or [WHOLE] * len(args),
        out_specs=WHOLE if single else [WHOLE] * len(outs),
        scratch_shapes=list(scratch),
        cost_estimate=pl.CostEstimate(flops=flops, bytes_accessed=moved, transcendentals=0),
        compiler_params=pltpu.CompilerParams(vmem_limit_bytes=16 << 20),
    )(*args)


def swap(block, axis, stride):
    count = lax.axis_size(axis)
    return lax.ppermute(block, axis, [(low, low ^ stride) for low in range(count)])


def own_and_other(part):
    me = lax.axis_index("row")
    return (
        pl.ds(pl.multiple_of(me * part, part), part),
        pl.ds(pl.multiple_of((1 - me) * part, part), part),
    )


def prepare(lower_0, lower_1, lower_2t, pattern, inv_1, inv_2, across, along):
    rows = lower_0.shape[1]
    blocks = pattern.shape[1]
    spread = rows // blocks
    size = lower_0.shape[2]
    n0, n1 = lower_0.shape[0], lower_1.shape[0]
    part_1, part_2 = lower_1.shape[2], lower_2t.shape[1]
    for b in range(blocks):
        at = pl.ds(b * spread, spread)
        for m in range(n0):
            factor = pattern[0, b, m].astype(BF16)
            across[at, pl.ds(m * size, size)] = lower_0[m, at, :] * factor
        for m in range(n1):
            factor = pattern[0, b, n0 + m].astype(BF16)
            masked = lower_1[m, at, :] * factor
            across[at, pl.ds(n0 * size + m * part_1, part_1)] = masked
            along[at, pl.ds(size + m * part_1, part_1)] = masked
    lane = lax.broadcasted_iota(jnp.int32, (1, rows), 1) // spread
    keep = jnp.zeros((1, rows), F32)
    for b in range(blocks):
        keep = jnp.where(lane == b, pattern[0, b, n0 + n1].astype(F32), keep)
    masked = (lower_2t[0].astype(F32) * keep).astype(BF16)
    start = n0 * size + n1 * part_1
    across[pl.ds(0, part_2), pl.ds(start, rows)] = masked
    across[pl.ds(part_2, rows - part_2), pl.ds(start, rows)] = jnp.zeros((rows - part_2, rows), BF16)
    along[pl.ds(0, part_1), pl.ds(0, size)] = inv_1[...]
    along[pl.ds(part_1, part_2), pl.ds(0, size)] = inv_2[...]
    along[pl.ds(part_1, part_2), pl.ds(size, rows)] = masked
    wide = along.shape[1] - size - rows
    along[pl.ds(part_1, part_2), pl.ds(size + rows, wide)] = jnp.zeros((part_2, wide), BF16)


def leaf_sums(solved, lower, rhs, keep, send, total, ready=None):
    leaves = lower.shape[1]
    mine, _ = own_and_other(rhs.shape[2])
    own, other = own_and_other(keep.shape[2])
    for m in range(keep.shape[0]):
        if ready:
            ready(m)
        acc = dot(lower[m, 0], solved[0])
        for v in range(1, leaves):
            acc = acc + dot(lower[m, v], solved[v])
        total[...] = -acc
        total[mine, :] = total[mine, :] + rhs[m, 0].astype(F32)
        keep[m] = total[:, own]
        send[m] = total[:, other].astype(BF16)


def opening(
    inverse, right, lower, rhs, lower_0, lower_1, lower_2t, pattern, inv_1, inv_2,
    solved, keep, send, across, along, lower_late, rhs_late,
    total, inverse_v, right_v, lower_v, rhs_v, low0_v, low1_v, low2_v, inv1_v, inv2_v, pattern_s, sems,
):
    leaves = inverse.shape[0]
    early = keep.shape[0]
    late = lower_late.shape[0]
    copies = []

    def fetch(source, target):
        copy = pltpu.make_async_copy(source, target, sems.at[len(copies)])
        copy.start()
        copies.append(copy)
        return copy

    leaf = []
    for v in range(leaves):
        leaf.append((fetch(inverse.at[v], inverse_v.at[v]), fetch(right.at[v], right_v.at[v])))
    sums = [fetch(lower.at[m], lower_v.at[m]) for m in range(early)]
    tops = fetch(rhs.at[pl.ds(0, early)], rhs_v)
    small = [
        fetch(source, target)
        for source, target in (
            (lower_0, low0_v), (lower_1, low1_v), (lower_2t, low2_v), (pattern, pattern_s),
            (inv_1, inv1_v), (inv_2, inv2_v),
        )
    ]
    last = [
        fetch(lower.at[pl.ds(early, late)], lower_late),
        fetch(rhs.at[pl.ds(early, late)], rhs_late),
    ]
    for v in range(leaves):
        for copy in leaf[v]:
            copy.wait()
        solved[v] = dot(inverse_v[v], right_v[v]).astype(BF16)
    tops.wait()
    leaf_sums(solved, lower_v, rhs_v, keep, send, total, lambda m: sums[m].wait())
    for copy in small:
        copy.wait()
    prepare(low0_v, low1_v, low2_v, pattern_s, inv1_v, inv2_v, across, along)
    for copy in last:
        copy.wait()


def leaf_b(solved, lower, rhs, keep, send, total):
    leaf_sums(solved, lower, rhs, keep, send, total)


def zero_a(keep, got, inverse, across, across_o, solved_out, p1):
    size = inverse.shape[1]
    residual = (keep[0] + got[0].astype(F32)).astype(BF16)
    solved = dot(inverse[...], residual).astype(BF16)
    solved_out[...] = solved
    for low, at in zip((across, across_o), own_and_other(across.shape[0])):
        total = keep[1, at, :] + got[1, at, :].astype(F32)
        p1[at, :] = (total - dot(low[:, pl.ds(0, size)], solved)).astype(BF16)


def zero_b(keep, got, solved, across, across_o, p2, p3):
    size = solved.shape[0]
    for low, at in zip((across, across_o), own_and_other(across.shape[0])):
        for m, out in enumerate((p2, p3)):
            total = keep[m, at, :] + got[m, at, :].astype(F32)
            low_m = low[:, pl.ds((m + 1) * size, size)]
            out[at, :] = (total - dot(low_m, solved[...])).astype(BF16)


def one(p1, p1_x, along, along_x, across_o, along_xo, solved_out, u2, u3):
    size = p1.shape[0]
    part = solved_out.shape[0]
    first = across_o.shape[1] - along_x.shape[1] + size - part
    residual = (p1[...].astype(F32) + p1_x[...].astype(F32)).astype(BF16)
    solved = dot(along[pl.ds(0, part), pl.ds(0, size)], residual).astype(BF16)
    solved_x = dot(along_x[pl.ds(0, part), pl.ds(0, size)], residual).astype(BF16)
    solved_out[...] = solved
    first = 3 * size
    mine, theirs = own_and_other(across_o.shape[0])
    for m, out in enumerate((u2, u3)):
        at = pl.ds(size + m * part, part)
        out[mine, :] = (
            dot(along[pl.ds(0, part), at], solved) + dot(along_x[pl.ds(0, part), at], solved_x)
        ).astype(BF16)
        out[theirs, :] = (
            dot(across_o[:, pl.ds(first + m * part, part)], solved)
            + dot(along_xo[pl.ds(0, part), at], solved_x)
        ).astype(BF16)


def two(s2, s2_x, u2, u2_y, along, along_x, side, across_o, along_xo, side_o, s3, s3_y, solved_out, v3):
    size = s2.shape[0]
    part = solved_out.shape[0]
    rows = across_o.shape[0]
    top = along.shape[0] - part
    residual = (
        s2[...].astype(F32) + s2_x[...].astype(F32) - (u2[...].astype(F32) + u2_y[...].astype(F32))
    ).astype(BF16)
    pieces = [(along, top), (along_x, top), (side, 0), (side, part)]
    others = [(across_o, 0, across_o.shape[1] - rows)] + [
        (ref, at, size) for ref, at in ((along_xo, top), (side_o, 0), (side_o, part))
    ]
    mine, theirs = own_and_other(rows)
    total = [s3[at, :].astype(F32) + s3_y[at, :].astype(F32) for at in (mine, theirs)]
    for i, ((ref, at), (ref_o, at_o, lane_o)) in enumerate(zip(pieces, others)):
        solved = dot(ref[pl.ds(at, part), pl.ds(0, size)], residual).astype(BF16)
        if i == 0:
            solved_out[...] = solved
        total[0] = total[0] - dot_t(ref[pl.ds(at, part), pl.ds(size, rows)], solved)
        total[1] = total[1] - dot_t(ref_o[pl.ds(at_o, part), pl.ds(lane_o, rows)], solved)
    v3[mine, :] = total[0].astype(BF16)
    v3[theirs, :] = total[1].astype(BF16)


def three(v3, v3_z, inverse, solved_out):
    residual = (v3[...].astype(F32) + v3_z[...].astype(F32)).astype(BF16)
    solved_out[...] = dot(inverse[...], residual).astype(BF16)


def add_2(a, b, out):
    out[...] = (a[...].astype(F32) + b[...].astype(F32)).astype(BF16)


def add_3(a, b, c, out):
    out[...] = (a[...].astype(F32) + b[...].astype(F32) - c[...].astype(F32)).astype(BF16)


def join(own, got, out):
    mine, theirs = own_and_other(own.shape[1])
    out[:, mine] = own[...]
    out[:, theirs] = got[...]


def body(
    rhs, leaf_rhs, leaf_inverse, leaf_lower,
    inverse_0, inverse_1, inverse_2, inverse_3,
    lower_0, lower_1, lower_2, sparsity,
):
    levels, _, rows, width = rhs.shape
    leaves, size, _ = leaf_inverse.shape
    half = width // lax.axis_size("row")
    n0, n1 = lower_0.shape[0], lower_1.shape[0]
    part_1, part_2 = inverse_1.shape[0], inverse_2.shape[0]
    block = ((size, half), BF16)
    full = [pltpu.VMEM((size, width), F32)]

    early = 2
    late = levels - early
    lower_2t, pattern = jnp.swapaxes(lower_2, 1, 2), jnp.transpose(sparsity, (1, 2, 0))
    sources = (leaf_inverse, leaf_rhs, leaf_lower, rhs, lower_0, lower_1, lower_2t, pattern, inverse_1, inverse_2)
    solved_leaf, keep_a, send_a, across, along, lower_late, rhs_late = call(
        opening,
        [
            ((leaves, size, width), BF16),
            ((early, size, half), F32),
            ((early, size, half), BF16),
            ((rows, n0 * size + n1 * part_1 + rows), BF16),
            ((part_1 + part_2, size + n1 * part_1), BF16),
            ((late, leaves, size, size), BF16),
            ((late, 1, rows, width), BF16),
        ],
        *(pltpu.with_memory_space_constraint(x, pltpu.HBM) for x in sources),
        specs=[pl.BlockSpec(memory_space=pltpu.HBM)] * len(sources),
        scratch=[pltpu.VMEM((size, width), F32)]
        + [pltpu.VMEM(x.shape, BF16) for x in (leaf_inverse, leaf_rhs)]
        + [pltpu.VMEM((early, *x.shape[1:]), BF16) for x in (leaf_lower, rhs)]
        + [pltpu.VMEM(x.shape, BF16) for x in (lower_0, lower_1, lower_2t, inverse_1, inverse_2)]
        + [pltpu.SMEM(pattern.shape, jnp.int32), pltpu.SemaphoreType.DMA((2 * leaves + early + 9,))],
        flops=6 * leaves * size * size * width,
    )
    got_a = swap(send_a, "row", 1)
    across_o = swap(across, "row", 1)
    along_x = swap(along, "col", 1)
    keep_b, send_b = call(
        leaf_b,
        [((late, size, half), F32), ((late, size, half), BF16)],
        solved_leaf, lower_late, rhs_late,
        scratch=full, flops=2 * late * leaves * size * size * width,
    )
    got_b = swap(send_b, "row", 1)
    sol0, p1 = call(
        zero_a, [block] * 2, keep_a, got_a, inverse_0, across, across_o,
        flops=4 * size * size * half,
    )
    p1_x = swap(p1, "col", 1)
    p2, p3 = call(
        zero_b, [block] * 2, keep_b, got_b, sol0, across, across_o,
        flops=4 * size * size * half,
    )
    p2_y = swap(p2, "col", 2)
    p3_x = swap(p3, "col", 1)
    along_xo = swap(along_x, "row", 1)
    side = swap(
        jnp.concatenate([along[part_1:, : size + rows], along_x[part_1:, : size + rows]]),
        "col", 2,
    )
    sol1, u2, u3 = call(
        one, [((part_1, half), BF16), block, block],
        p1, p1_x, along, along_x, across_o, along_xo,
        flops=6 * size * size * half,
    )
    u2_y = swap(u2, "col", 2)
    s2 = call(add_2, [block], p2, p2_y)
    s2_x = swap(s2, "col", 1)
    s3 = call(add_3, [block], p3, p3_x, u3)
    s3_y = swap(s3, "col", 2)
    side_o = swap(side, "row", 1)
    sol2, v3 = call(
        two, [((part_2, half), BF16), block],
        s2, s2_x, u2, u2_y, along, along_x, side, across_o, along_xo, side_o, s3, s3_y,
        flops=4 * size * size * half,
    )
    v3_z = swap(v3, "col", 4)
    sol3 = call(
        three, [((inverse_3.shape[0], half), BF16)], v3, v3_z, inverse_3,
        flops=2 * inverse_3.size * half,
    )
    outs = []
    for solved in (sol0, sol1, sol2, sol3):
        got = swap(solved, "row", 1)
        outs.append(call(join, [((solved.shape[0], width), BF16)], solved, got))
    return tuple(outs)


def solution(mesh):
    return jax.shard_map(
        body,
        mesh=mesh,
        in_specs=(
            P(None, "col", "row", None),
            P(("col", "row"), None, None),
            P(("col", "row"), None, None),
            P(None, ("col", "row"), None, None),
            P("col", None),
            P("col", None),
            P("col", None),
            P("col", None),
            P(None, "row", "col"),
            P(None, "row", "col"),
            P(None, "row", "col"),
            P(None, "col", "row"),
        ),
        out_specs=(P("col", None), P("col", None), P("col", None), P("col", None)),
        check_vma=False,
    )
```

```python
import jax
import jax.numpy as jnp
from jax import lax
from jax.experimental import pallas as pl
from jax.experimental.pallas import tpu as pltpu
from jax.sharding import PartitionSpec as P

F32, BF16 = jnp.float32, jnp.bfloat16
WHOLE = pl.BlockSpec(memory_space=pltpu.VMEM)
SCALARS = pl.BlockSpec(memory_space=pltpu.SMEM)


def dot(a, b):
    return jnp.dot(a, b, preferred_element_type=F32)


def dot_t(a, b):
    return lax.dot_general(a, b, (((0,), (0,)), ((), ())), preferred_element_type=F32)


def call(kernel, outs, *args, scratch=(), flops=0, specs=None):
    outs = [jax.ShapeDtypeStruct(shape, dtype) for shape, dtype in outs]
    moved = sum(a.size * a.dtype.itemsize for a in (*args, *outs))
    single = len(outs) == 1
    return pl.pallas_call(
        kernel,
        out_shape=outs[0] if single else outs,
        in_specs=specs or [WHOLE] * len(args),
        out_specs=WHOLE if single else [WHOLE] * len(outs),
        scratch_shapes=list(scratch),
        cost_estimate=pl.CostEstimate(flops=flops, bytes_accessed=moved, transcendentals=0),
        compiler_params=pltpu.CompilerParams(vmem_limit_bytes=16 << 20),
    )(*args)


def swap(block, axis, stride):
    count = lax.axis_size(axis)
    return lax.ppermute(block, axis, [(low, low ^ stride) for low in range(count)])


def own_and_other(part):
    me = lax.axis_index("row")
    return (
        pl.ds(pl.multiple_of(me * part, part), part),
        pl.ds(pl.multiple_of((1 - me) * part, part), part),
    )


def prepare(lower_0, lower_1, lower_2t, pattern, inv_1, inv_2, across, along_1, along_2):
    rows = lower_0.shape[1]
    blocks = pattern.shape[1]
    spread = rows // blocks
    size = lower_0.shape[2]
    n0, n1 = lower_0.shape[0], lower_1.shape[0]
    part_1, part_2 = lower_1.shape[2], lower_2t.shape[1]
    for b in range(blocks):
        at = pl.ds(b * spread, spread)
        for m in range(n0):
            factor = pattern[0, b, m].astype(BF16)
            across[at, pl.ds(m * size, size)] = lower_0[m, at, :] * factor
        for m in range(n1):
            factor = pattern[0, b, n0 + m].astype(BF16)
            masked = lower_1[m, at, :] * factor
            across[at, pl.ds(n0 * size + m * part_1, part_1)] = masked
            along_1[at, pl.ds(m * part_1, part_1)] = masked
    lane = lax.broadcasted_iota(jnp.int32, (1, rows), 1) // spread
    keep = jnp.zeros((1, rows), F32)
    for b in range(blocks):
        keep = jnp.where(lane == b, pattern[0, b, n0 + n1].astype(F32), keep)
    masked = (lower_2t[0].astype(F32) * keep).astype(BF16)
    start = n0 * size + n1 * part_1
    across[pl.ds(0, part_2), pl.ds(start, rows)] = masked
    across[pl.ds(part_2, rows - part_2), pl.ds(start, rows)] = jnp.zeros((rows - part_2, rows), BF16)
    cut = along_1.shape[0] - rows
    mine, _ = own_and_other(cut)
    along_1[pl.ds(rows, cut), :] = inv_1[mine, :]
    along_2[:, pl.ds(0, size)] = inv_2[...]
    along_2[:, pl.ds(size, rows)] = masked


def leaf_sums(solved, lower, rhs, keep, send, total, ready=None):
    leaves = lower.shape[1]
    mine, _ = own_and_other(rhs.shape[2])
    own, other = own_and_other(keep.shape[2])
    for m in range(keep.shape[0]):
        if ready:
            ready(m)
        acc = dot(lower[m, 0], solved[0])
        for v in range(1, leaves):
            acc = acc + dot(lower[m, v], solved[v])
        total[...] = -acc
        total[mine, :] = total[mine, :] + rhs[m, 0].astype(F32)
        keep[m] = total[:, own]
        send[m] = total[:, other].astype(BF16)


def opening(
    inverse, right, lower, rhs, lower_0, lower_1, lower_2t, pattern, inv_1, inv_2,
    solved, keep, send, across, along_1, along_2, lower_late, rhs_late,
    total, inverse_v, right_v, lower_v, rhs_v, low0_v, low1_v, low2_v, inv1_v, inv2_v, pattern_s, sems,
):
    leaves = inverse.shape[0]
    early = keep.shape[0]
    late = lower_late.shape[0]
    copies = []

    def fetch(source, target):
        copy = pltpu.make_async_copy(source, target, sems.at[len(copies)])
        copy.start()
        copies.append(copy)
        return copy

    leaf = []
    for v in range(leaves):
        leaf.append((fetch(inverse.at[v], inverse_v.at[v]), fetch(right.at[v], right_v.at[v])))
    sums = [fetch(lower.at[m], lower_v.at[m]) for m in range(early)]
    tops = fetch(rhs.at[pl.ds(0, early)], rhs_v)
    small = [
        fetch(source, target)
        for source, target in (
            (lower_0, low0_v), (lower_1, low1_v), (lower_2t, low2_v), (pattern, pattern_s),
            (inv_1, inv1_v), (inv_2, inv2_v),
        )
    ]
    last = [
        fetch(lower.at[pl.ds(early, late)], lower_late),
        fetch(rhs.at[pl.ds(early, late)], rhs_late),
    ]
    for v in range(leaves):
        for copy in leaf[v]:
            copy.wait()
        solved[v] = dot(inverse_v[v], right_v[v]).astype(BF16)
    tops.wait()
    leaf_sums(solved, lower_v, rhs_v, keep, send, total, lambda m: sums[m].wait())
    for copy in small:
        copy.wait()
    prepare(low0_v, low1_v, low2_v, pattern_s, inv1_v, inv2_v, across, along_1, along_2)
    for copy in last:
        copy.wait()


def leaf_b(solved, lower, rhs, keep, send, total):
    leaf_sums(solved, lower, rhs, keep, send, total)


def quarters(half):
    part = half // 2
    bit = lax.rem(lax.axis_index("col"), 2)
    return (
        pl.ds(pl.multiple_of(bit * part, part), part),
        pl.ds(pl.multiple_of((1 - bit) * part, part), part),
    )


def zero_a(keep, got, inverse, across, across_o, solved_out, kept, sent, total):
    size = inverse.shape[1]
    residual = (keep[0] + got[0].astype(F32)).astype(BF16)
    solved = dot(inverse[...], residual).astype(BF16)
    solved_out[...] = solved
    for low, at in zip((across, across_o), own_and_other(across.shape[0])):
        before = keep[1, at, :] + got[1, at, :].astype(F32)
        total[at, :] = before - dot(low[:, pl.ds(0, size)], solved)
    own, other = quarters(total.shape[1])
    kept[...] = total[:, own]
    sent[...] = total[:, other].astype(BF16)


def zero_b(keep, got, solved, across, across_o, kept_2, sent_2, kept_3, sent_3, total):
    size = solved.shape[0]
    own, other = quarters(total.shape[1])
    for m, (kept, sent) in enumerate(((kept_2, sent_2), (kept_3, sent_3))):
        for low, at in zip((across, across_o), own_and_other(across.shape[0])):
            before = keep[m, at, :] + got[m, at, :].astype(F32)
            total[at, :] = before - dot(low[:, pl.ds((m + 1) * size, size)], solved[...])
        kept[...] = total[:, own]
        sent[...] = total[:, other].astype(BF16)


def one(kept, got, inverse, along, along_x, across_o, along_xo, solved_own, solved_x, u2, u3):
    size, part = kept.shape[0], inverse.shape[0]
    rows = across_o.shape[0]
    residual = (kept[...] + got[...].astype(F32)).astype(BF16)
    solved_own[...] = dot(inverse[...], residual).astype(BF16)
    cut = along.shape[0] - rows
    for ref, at in zip((along_x, along_xo), own_and_other(cut)):
        solved_x[at, :] = dot(ref[pl.ds(rows, cut), :], residual).astype(BF16)
    own, other = solved_own[...], solved_x[...]
    first = 3 * size
    mine, theirs = own_and_other(rows)
    for m, out in enumerate((u2, u3)):
        at = pl.ds(m * part, part)
        out[mine, :] = dot(along[pl.ds(0, rows), at], own) + dot(along_x[pl.ds(0, rows), at], other)
        out[theirs, :] = dot(across_o[:, pl.ds(first + m * part, part)], own) + dot(
            along_xo[pl.ds(0, rows), at], other
        )


def difference(kept, got, update, out):
    out[...] = (kept[...] + got[...].astype(F32) - update[...]).astype(BF16)


def two(w2, w2_y, along, along_x, side, across_o, along_xo, side_o, s3, s3_y, solved_own, solved_x, v3):
    part = along.shape[0]
    size = w2.shape[0]
    rows = across_o.shape[0]
    residual = (w2[...].astype(F32) + w2_y[...].astype(F32)).astype(BF16)
    pieces = ((along, 0), (along_x, 0), (side, 0), (side, part))
    others = (
        (across_o, 0, across_o.shape[1] - rows), (along_xo, 0, size), (side_o, 0, size), (side_o, part, size),
    )
    mine, theirs = own_and_other(rows)
    total = [s3[at, :].astype(F32) + s3_y[at, :].astype(F32) for at in (mine, theirs)]
    for i, ((ref, at), (ref_o, at_o, lane_o)) in enumerate(zip(pieces, others)):
        solved = dot(ref[pl.ds(at, part), pl.ds(0, size)], residual).astype(BF16)
        if i < 2:
            (solved_own, solved_x)[i][...] = solved
        total[0] = total[0] - dot_t(ref[pl.ds(at, part), pl.ds(size, rows)], solved)
        total[1] = total[1] - dot_t(ref_o[pl.ds(at_o, part), pl.ds(lane_o, rows)], solved)
    v3[mine, :] = total[0].astype(BF16)
    v3[theirs, :] = total[1].astype(BF16)


def three(v3, v3_x, v3_z, v3_xz, inverse, sol1, sol1_x, sol2, sol2_x, out, full):
    own, other = quarters(out.shape[1])
    full[:, own] = (v3[...].astype(F32) + v3_z[...].astype(F32)).astype(BF16)
    full[:, other] = (v3_x[...].astype(F32) + v3_xz[...].astype(F32)).astype(BF16)
    n1, n2 = sol1.shape[0], sol2.shape[0]
    out[pl.ds(0, n1), own] = sol1[...]
    out[pl.ds(0, n1), other] = sol1_x[...]
    out[pl.ds(n1, n2), own] = sol2[...]
    out[pl.ds(n1, n2), other] = sol2_x[...]
    out[pl.ds(n1 + n2, inverse.shape[0]), :] = dot(inverse[...], full[...]).astype(BF16)


def join(own, got, *outs):
    mine, theirs = own_and_other(own.shape[1])
    first = 0
    for out in outs:
        at = pl.ds(first, out.shape[0])
        out[:, mine] = own[at, :]
        out[:, theirs] = got[at, :]
        first += out.shape[0]


def body(
    rhs, leaf_rhs, leaf_inverse, leaf_lower,
    inverse_0, inverse_1, inverse_2, inverse_3,
    lower_0, lower_1, lower_2, sparsity,
):
    levels, _, rows, width = rhs.shape
    leaves, size, _ = leaf_inverse.shape
    half = width // lax.axis_size("row")
    n0, n1 = lower_0.shape[0], lower_1.shape[0]
    part_1, part_2 = inverse_1.shape[0], inverse_2.shape[0]
    full = [pltpu.VMEM((size, width), F32)]

    early = 2
    late = levels - early
    lower_2t, pattern = jnp.swapaxes(lower_2, 1, 2), jnp.transpose(sparsity, (1, 2, 0))
    sources = (leaf_inverse, leaf_rhs, leaf_lower, rhs, lower_0, lower_1, lower_2t, pattern, inverse_1, inverse_2)
    solved_leaf, keep_a, send_a, across, along_1, along_2, lower_late, rhs_late = call(
        opening,
        [
            ((leaves, size, width), BF16),
            ((early, size, half), F32),
            ((early, size, half), BF16),
            ((rows, n0 * size + n1 * part_1 + rows), BF16),
            ((rows + part_1 // 2, n1 * part_1), BF16),
            ((part_2, size + rows), BF16),
            ((late, leaves, size, size), BF16),
            ((late, 1, rows, width), BF16),
        ],
        *(pltpu.with_memory_space_constraint(x, pltpu.HBM) for x in sources),
        specs=[pl.BlockSpec(memory_space=pltpu.HBM)] * len(sources),
        scratch=[pltpu.VMEM((size, width), F32)]
        + [pltpu.VMEM(x.shape, BF16) for x in (leaf_inverse, leaf_rhs)]
        + [pltpu.VMEM((early, *x.shape[1:]), BF16) for x in (leaf_lower, rhs)]
        + [pltpu.VMEM(x.shape, BF16) for x in (lower_0, lower_1, lower_2t, inverse_1, inverse_2)]
        + [pltpu.SMEM(pattern.shape, jnp.int32), pltpu.SemaphoreType.DMA((2 * leaves + early + 9,))],
        flops=6 * leaves * size * size * width,
    )
    got_a = swap(send_a, "row", 1)
    across_o = swap(across, "row", 1)
    along_2x = swap(along_2, "col", 1)
    along_1x = swap(along_1, "col", 1)
    keep_b, send_b = call(
        leaf_b,
        [((late, size, half), F32), ((late, size, half), BF16)],
        solved_leaf, lower_late, rhs_late,
        scratch=full, flops=2 * late * leaves * size * size * width,
    )
    got_b = swap(send_b, "row", 1)
    quarter = half // 2
    square = pltpu.VMEM((size, half), F32)
    kept, sent = ((size, quarter), F32), ((size, quarter), BF16)
    sol0, kept1, sent1 = call(
        zero_a, [((size, half), BF16), kept, sent], keep_a, got_a, inverse_0, across, across_o,
        scratch=[square], flops=4 * size * size * half,
    )
    got1 = swap(sent1, "col", 1)
    kept2, sent2, kept3, sent3 = call(
        zero_b, [kept, sent, kept, sent], keep_b, got_b, sol0, across, across_o,
        scratch=[square], flops=4 * size * size * half,
    )
    got2 = swap(sent2, "col", 1)
    side = swap(jnp.concatenate([along_2, along_2x]), "col", 2)
    got3 = swap(sent3, "col", 1)
    along_2xo = swap(along_2x, "row", 1)
    along_1xo = swap(along_1x, "row", 1)
    sol1, sol1_for_x, u2, u3 = call(
        one, [((part_1, quarter), BF16)] * 2 + [kept] * 2,
        kept1, got1, inverse_1, along_1, along_1x, across_o, along_1xo,
        flops=6 * size * size * quarter,
    )
    w2 = call(difference, [sent], kept2, got2, u2)
    w2_y = swap(w2, "col", 2)
    sol0_o = swap(sol0, "row", 1)
    side_o = swap(side, "row", 1)
    s3 = call(difference, [sent], kept3, got3, u3)
    s3_y = swap(s3, "col", 2)
    out0 = call(join, [((size, width), BF16)], sol0, sol0_o)
    sol2, sol2_for_x, v3 = call(
        two, [((part_2, quarter), BF16)] * 2 + [sent],
        w2, w2_y, along_2, along_2x, side, across_o, along_2xo, side_o, s3, s3_y,
        flops=4 * size * size * quarter,
    )
    v3_xz = swap(v3, "col", 5)
    v3_x = swap(v3, "col", 1)
    v3_z = swap(v3, "col", 4)
    sol1_x = swap(sol1_for_x, "col", 1)
    sol2_x = swap(sol2_for_x, "col", 1)
    part_3 = inverse_3.shape[0]
    last = call(
        three, [((part_1 + part_2 + part_3, half), BF16)],
        v3, v3_x, v3_z, v3_xz, inverse_3, sol1, sol1_x, sol2, sol2_x,
        scratch=[pltpu.VMEM((size, half), BF16)], flops=2 * inverse_3.size * half,
    )
    last_o = swap(last, "row", 1)
    rest = call(join, [((part, width), BF16) for part in (part_1, part_2, part_3)], last, last_o)
    return (out0, *rest)


def solution(mesh):
    return jax.shard_map(
        body,
        mesh=mesh,
        in_specs=(
            P(None, "col", "row", None),
            P(("col", "row"), None, None),
            P(("col", "row"), None, None),
            P(None, ("col", "row"), None, None),
            P("col", None),
            P("col", None),
            P("col", None),
            P("col", None),
            P(None, "row", "col"),
            P(None, "row", "col"),
            P(None, "row", "col"),
            P(None, "col", "row"),
        ),
        out_specs=(P("col", None), P("col", None), P("col", None), P("col", None)),
        check_vma=False,
    )
```

```python
import jax
import jax.numpy as jnp
from jax import lax
from jax.experimental import pallas as pl
from jax.experimental.pallas import tpu as pltpu
from jax.sharding import PartitionSpec as P

F32, BF16 = jnp.float32, jnp.bfloat16
WHOLE = pl.BlockSpec(memory_space=pltpu.VMEM)
SCALARS = pl.BlockSpec(memory_space=pltpu.SMEM)


def dot(a, b):
    return jnp.dot(a, b, preferred_element_type=F32)


def dot_t(a, b):
    return lax.dot_general(a, b, (((0,), (0,)), ((), ())), preferred_element_type=F32)


def call(kernel, outs, *args, scratch=(), flops=0, specs=None):
    outs = [jax.ShapeDtypeStruct(shape, dtype) for shape, dtype in outs]
    moved = sum(a.size * a.dtype.itemsize for a in (*args, *outs))
    single = len(outs) == 1
    return pl.pallas_call(
        kernel,
        out_shape=outs[0] if single else outs,
        in_specs=specs or [WHOLE] * len(args),
        out_specs=WHOLE if single else [WHOLE] * len(outs),
        scratch_shapes=list(scratch),
        cost_estimate=pl.CostEstimate(flops=flops, bytes_accessed=moved, transcendentals=0),
        compiler_params=pltpu.CompilerParams(vmem_limit_bytes=16 << 20),
    )(*args)


def swap(block, axis, stride):
    count = lax.axis_size(axis)
    return lax.ppermute(block, axis, [(low, low ^ stride) for low in range(count)])


def own_and_other(part):
    me = lax.axis_index("row")
    return (
        pl.ds(pl.multiple_of(me * part, part), part),
        pl.ds(pl.multiple_of((1 - me) * part, part), part),
    )


def prepare(lower_0, lower_1, lower_2t, pattern, inv_1, inv_2, pack, first, along):
    rows = lower_0.shape[1]
    blocks = pattern.shape[1]
    spread = rows // blocks
    n0, n1 = lower_0.shape[0], lower_1.shape[0]
    part_1, part_2 = lower_1.shape[2], lower_2t.shape[1]
    for b in range(blocks):
        at = pl.ds(b * spread, spread)
        for m in range(n0):
            factor = pattern[0, b, m].astype(BF16)
            pack[pl.ds(first + m * rows + b * spread, spread), :] = lower_0[m, at, :] * factor
        for m in range(n1):
            factor = pattern[0, b, n0 + m].astype(BF16)
            masked = lower_1[m, at, :] * factor
            lanes = pl.ds(m * part_1, part_1)
            pack[pl.ds(first + n0 * rows + b * spread, spread), lanes] = masked
            along[at, lanes] = masked
    lane = lax.broadcasted_iota(jnp.int32, (1, rows), 1) // spread
    keep = jnp.zeros((1, rows), F32)
    for b in range(blocks):
        keep = jnp.where(lane == b, pattern[0, b, n0 + n1].astype(F32), keep)
    short = part_2 // 2
    cut = part_1 // 2
    last = rows + cut + part_2
    for i in range(2):
        masked = (lower_2t[0, pl.ds(i * short, short), :].astype(F32) * keep).astype(BF16)
        pack[pl.ds(first + (n0 + 1) * rows, short), pl.ds(i * rows, rows)] = masked
        along[pl.ds(last, short), pl.ds(i * rows, rows)] = masked
    mine, _ = own_and_other(cut)
    along[pl.ds(rows, cut), :] = inv_1[mine, :]
    along[pl.ds(rows + cut, part_2), :] = inv_2[...]


def leaf_sum(m, solved, lower, rhs, keep, send, total):
    leaves = lower.shape[1]
    mine, _ = own_and_other(rhs.shape[2])
    own, other = own_and_other(keep.shape[2])
    acc = dot(lower[m, 0], solved[0])
    for v in range(1, leaves):
        acc = acc + dot(lower[m, v], solved[v])
    total[...] = -acc
    total[mine, :] = total[mine, :] + rhs[m, 0].astype(F32)
    keep[m] = total[:, own]
    size = total.shape[0]
    send[pl.ds(m * size, size), :] = total[:, other].astype(BF16)


def opening(
    inverse, right, lower, rhs, lower_0, lower_1, lower_2t, pattern, inv_1, inv_2,
    solved, keep, pack, along, lower_late, rhs_late,
    total, inverse_v, right_v, lower_v, rhs_v, low0_v, low1_v, low2_v, inv1_v, inv2_v, pattern_s, sems,
):
    leaves, size, _ = inverse.shape
    early = keep.shape[0]
    late = lower_late.shape[0]
    copies = []

    def fetch(source, target):
        copy = pltpu.make_async_copy(source, target, sems.at[len(copies)])
        copy.start()
        copies.append(copy)
        return copy

    leaf = []
    for v in range(leaves):
        leaf.append((fetch(inverse.at[v], inverse_v.at[v]), fetch(right.at[v], right_v.at[v])))
    sums = [fetch(lower.at[0], lower_v.at[0]), fetch(rhs.at[pl.ds(0, early)], rhs_v)]
    small = [
        fetch(source, target)
        for source, target in (
            (lower_0, low0_v), (lower_1, low1_v), (lower_2t, low2_v), (pattern, pattern_s),
            (inv_1, inv1_v), (inv_2, inv2_v),
        )
    ]
    small += [fetch(lower.at[m], lower_v.at[m]) for m in range(1, early)]
    last = [
        fetch(lower.at[pl.ds(early, late)], lower_late),
        fetch(rhs.at[pl.ds(early, late)], rhs_late),
    ]
    for v in range(leaves):
        for copy in leaf[v]:
            copy.wait()
        solved[v] = dot(inverse_v[v], right_v[v]).astype(BF16)
    for copy in sums:
        copy.wait()
    leaf_sum(0, solved, lower_v, rhs_v, keep, pack, total)
    for copy in small:
        copy.wait()
    prepare(low0_v, low1_v, low2_v, pattern_s, inv1_v, inv2_v, pack, early * size, along)
    for m in range(1, early):
        leaf_sum(m, solved, lower_v, rhs_v, keep, pack, total)
    for copy in last:
        copy.wait()


def leaf_b(solved, lower, rhs, keep, send, total):
    for m in range(lower.shape[0]):
        leaf_sum(m, solved, lower, rhs, keep, send, total)


def quarters(half):
    part = half // 2
    bit = lax.rem(lax.axis_index("col"), 2)
    return (
        pl.ds(pl.multiple_of(bit * part, part), part),
        pl.ds(pl.multiple_of((1 - bit) * part, part), part),
    )


def zero_a(keep, pack, pack_o, inverse, solved_out, kept, sent, total):
    size = inverse.shape[1]
    rows = size // 2
    early = keep.shape[0]
    residual = (keep[0] + pack_o[pl.ds(0, size), :].astype(F32)).astype(BF16)
    solved = dot(inverse[...], residual).astype(BF16)
    solved_out[...] = solved
    total[...] = keep[1] + pack_o[pl.ds(size, size), :].astype(F32)
    for ref, at in zip((pack, pack_o), own_and_other(rows)):
        total[at, :] = total[at, :] - dot(ref[pl.ds(early * size, rows), :], solved)
    own, other = quarters(total.shape[1])
    kept[...] = total[:, own]
    sent[...] = total[:, other].astype(BF16)


def zero_b(keep, got, solved, pack, pack_o, kept, sent, total):
    size = solved.shape[0]
    rows = size // 2
    first = 2 * size + rows
    own, other = quarters(total.shape[1])
    for m in range(keep.shape[0]):
        total[...] = keep[m] + got[pl.ds(m * size, size), :].astype(F32)
        for ref, at in zip((pack, pack_o), own_and_other(rows)):
            total[at, :] = total[at, :] - dot(ref[pl.ds(first + m * rows, rows), :], solved[...])
        kept[m] = total[:, own]
        sent[m] = total[:, other].astype(BF16)


def one(kept, got, inverse, pack, pack_o, along, along_x, along_xo, solved_own, solved_x, u):
    size, part = kept.shape[0], inverse.shape[0]
    rows = size // 2
    first = 2 * size + 3 * rows
    residual = (kept[...] + got[...].astype(F32)).astype(BF16)
    solved_own[...] = dot(inverse[...], residual).astype(BF16)
    cut = part // 2
    for ref, at in zip((along_x, along_xo), own_and_other(cut)):
        solved_x[at, :] = dot(ref[pl.ds(rows, cut), :], residual).astype(BF16)
    own, other = solved_own[...], solved_x[...]
    for m in range(u.shape[0]):
        lanes = pl.ds(m * part, part)
        for ref, ref_x, at in zip((pack, pack_o), (along_x, along_xo), own_and_other(rows)):
            u[m, at, :] = dot(ref[pl.ds(first, rows), lanes], own) + dot(ref_x[pl.ds(0, rows), lanes], other)


def stack(along, along_x, out):
    part = out.shape[0] // 2
    at = pl.ds(along.shape[0] - part, part)
    out[pl.ds(0, part), :] = along[at, :]
    out[pl.ds(part, part), :] = along_x[at, :]


def differences(kept, got, update, out):
    out[...] = (kept[...] + got[...].astype(F32) - update[...]).astype(BF16)


def two(w, w_y, pack, pack_o, along, along_x, along_xo, side, side_o, sol1_x, solved_own, v3, to_x):
    size = w.shape[1]
    rows = size // 2
    part = solved_own.shape[0]
    short = part // 2
    residual = (w[0].astype(F32) + w_y[0].astype(F32)).astype(BF16)
    top = along.shape[0] - part - short
    step = part + short
    inverses = ((along, top), (along_x, top), (side, 0), (side, step))
    mine_at = ((along, top + part), (along_x, top + part), (side, part), (side, step + part))
    their_at = (
        (pack_o, pack_o.shape[0] - short), (along_xo, top + part), (side_o, part), (side_o, step + part),
    )
    ranges = own_and_other(rows)
    total = [w[1, at, :].astype(F32) + w_y[1, at, :].astype(F32) for at in ranges]
    for i, (ref, at) in enumerate(inverses):
        solved = dot(ref[pl.ds(at, part), :], residual).astype(BF16)
        if i == 0:
            solved_own[...] = solved
        if i == 1:
            to_x[pl.ds(size + rows, part), :] = solved
        for j, (low, start) in enumerate((mine_at[i], their_at[i])):
            block = low[pl.ds(start, short), :]
            total[j] = total[j] - dot_t(block[:, :rows], solved[:short]) - dot_t(block[:, rows:], solved[short:])
    for at, value in zip(ranges, total):
        v3[at, :] = value.astype(BF16)
        to_x[at, :] = value.astype(BF16)
    to_x[pl.ds(size, rows), :] = sol1_x[...]


def three(v3, v3_z, v3_xz, from_x, inverse, sol1, sol2, out, full):
    size = v3.shape[0]
    own, other = quarters(out.shape[1])
    full[:, own] = (v3[...].astype(F32) + v3_z[...].astype(F32)).astype(BF16)
    full[:, other] = (from_x[pl.ds(0, size), :].astype(F32) + v3_xz[...].astype(F32)).astype(BF16)
    n1, n2 = sol1.shape[0], sol2.shape[0]
    out[pl.ds(0, n1), own] = sol1[...]
    out[pl.ds(n1, n2), own] = sol2[...]
    out[pl.ds(0, n1 + n2), other] = from_x[pl.ds(size, n1 + n2), :]
    out[pl.ds(n1 + n2, inverse.shape[0]), :] = dot(inverse[...], full[...]).astype(BF16)


def join(own, got, *outs):
    mine, theirs = own_and_other(own.shape[1])
    first = 0
    for out in outs:
        at = pl.ds(first, out.shape[0])
        out[:, mine] = own[at, :]
        out[:, theirs] = got[at, :]
        first += out.shape[0]


def body(
    rhs, leaf_rhs, leaf_inverse, leaf_lower,
    inverse_0, inverse_1, inverse_2, inverse_3,
    lower_0, lower_1, lower_2, sparsity,
):
    levels, _, rows, width = rhs.shape
    leaves, size, _ = leaf_inverse.shape
    half = width // lax.axis_size("row")
    n0 = lower_0.shape[0]
    part_1, part_2 = inverse_1.shape[0], inverse_2.shape[0]
    full = [pltpu.VMEM((size, width), F32)]

    early = 2
    late = levels - early
    lower_2t, pattern = jnp.swapaxes(lower_2, 1, 2), jnp.transpose(sparsity, (1, 2, 0))
    sources = (leaf_inverse, leaf_rhs, leaf_lower, rhs, lower_0, lower_1, lower_2t, pattern, inverse_1, inverse_2)
    short = part_2 // 2
    solved_leaf, keep_a, pack, along, lower_late, rhs_late = call(
        opening,
        [
            ((leaves, size, width), BF16),
            ((early, size, half), F32),
            ((early * size + (n0 + 1) * rows + short, half), BF16),
            ((rows + part_1 // 2 + part_2 + short, half), BF16),
            ((late, leaves, size, size), BF16),
            ((late, 1, rows, width), BF16),
        ],
        *(pltpu.with_memory_space_constraint(x, pltpu.HBM) for x in sources),
        specs=[pl.BlockSpec(memory_space=pltpu.HBM)] * len(sources),
        scratch=[pltpu.VMEM((size, width), F32)]
        + [pltpu.VMEM(x.shape, BF16) for x in (leaf_inverse, leaf_rhs)]
        + [pltpu.VMEM((early, *x.shape[1:]), BF16) for x in (leaf_lower, rhs)]
        + [pltpu.VMEM(x.shape, BF16) for x in (lower_0, lower_1, lower_2t, inverse_1, inverse_2)]
        + [pltpu.SMEM(pattern.shape, jnp.int32), pltpu.SemaphoreType.DMA((2 * leaves + early + 9,))],
        flops=6 * leaves * size * size * width,
    )
    pack_o = swap(pack, "row", 1)
    along_x = swap(along, "col", 1)
    keep_b, send_b = call(
        leaf_b,
        [((late, size, half), F32), ((late * size, half), BF16)],
        solved_leaf, lower_late, rhs_late,
        scratch=full, flops=2 * late * leaves * size * size * width,
    )
    got_b = swap(send_b, "row", 1)
    quarter = half // 2
    square = pltpu.VMEM((size, half), F32)
    sol0, kept1, sent1 = call(
        zero_a, [((size, half), BF16), ((size, quarter), F32), ((size, quarter), BF16)],
        keep_a, pack, pack_o, inverse_0,
        scratch=[square], flops=4 * size * size * half,
    )
    got1 = swap(sent1, "col", 1)
    kept23, sent23 = call(
        zero_b, [((late, size, quarter), F32), ((late, size, quarter), BF16)],
        keep_b, got_b, sol0, pack, pack_o,
        scratch=[square], flops=4 * size * size * half,
    )
    got23 = swap(sent23, "col", 1)
    along_xo = swap(along_x, "row", 1)
    side = swap(call(stack, [((2 * (part_2 + short), half), BF16)], along, along_x), "col", 2)
    sol1, sol1_for_x, u = call(
        one, [((part_1, quarter), BF16)] * 2 + [((late, size, quarter), F32)],
        kept1, got1, inverse_1, pack, pack_o, along, along_x, along_xo,
        flops=6 * size * size * quarter,
    )
    w = call(differences, [((late, size, quarter), BF16)], kept23, got23, u)
    w_y = swap(w, "col", 2)
    sol0_o = swap(sol0, "row", 1)
    side_o = swap(side, "row", 1)
    out0 = call(join, [((size, width), BF16)], sol0, sol0_o)
    sol2, v3, to_x = call(
        two,
        [((part_2, quarter), BF16), ((size, quarter), BF16), ((size + part_1 + part_2, quarter), BF16)],
        w, w_y, pack, pack_o, along, along_x, along_xo, side, side_o, sol1_for_x,
        flops=4 * size * size * quarter,
    )
    v3_xz = swap(v3, "col", 5)
    from_x = swap(to_x, "col", 1)
    v3_z = swap(v3, "col", 4)
    part_3 = inverse_3.shape[0]
    last = call(
        three, [((part_1 + part_2 + part_3, half), BF16)],
        v3, v3_z, v3_xz, from_x, inverse_3, sol1, sol2,
        scratch=[pltpu.VMEM((size, half), BF16)], flops=2 * inverse_3.size * half,
    )
    last_o = swap(last, "row", 1)
    rest = call(join, [((part, width), BF16) for part in (part_1, part_2, part_3)], last, last_o)
    return (out0, *rest)


def solution(mesh):
    return jax.shard_map(
        body,
        mesh=mesh,
        in_specs=(
            P(None, "col", "row", None),
            P(("col", "row"), None, None),
            P(("col", "row"), None, None),
            P(None, ("col", "row"), None, None),
            P("col", None),
            P("col", None),
            P("col", None),
            P("col", None),
            P(None, "row", "col"),
            P(None, "row", "col"),
            P(None, "row", "col"),
            P(None, "col", "row"),
        ),
        out_specs=(P("col", None), P("col", None), P("col", None), P("col", None)),
        check_vma=False,
    )
```

```python
import jax
import jax.numpy as jnp
from jax import lax
from jax.experimental import pallas as pl
from jax.experimental.pallas import tpu as pltpu
from jax.sharding import PartitionSpec as P

F32, BF16 = jnp.float32, jnp.bfloat16
WHOLE = pl.BlockSpec(memory_space=pltpu.VMEM)
SCALARS = pl.BlockSpec(memory_space=pltpu.SMEM)


def dot(a, b):
    return jnp.dot(a, b, preferred_element_type=F32)


def dot_t(a, b):
    return lax.dot_general(a, b, (((0,), (0,)), ((), ())), preferred_element_type=F32)


def call(kernel, outs, *args, scratch=(), flops=0, specs=None):
    outs = [jax.ShapeDtypeStruct(shape, dtype) for shape, dtype in outs]
    moved = sum(a.size * a.dtype.itemsize for a in (*args, *outs))
    single = len(outs) == 1
    return pl.pallas_call(
        kernel,
        out_shape=outs[0] if single else outs,
        in_specs=specs or [WHOLE] * len(args),
        out_specs=WHOLE if single else [WHOLE] * len(outs),
        scratch_shapes=list(scratch),
        cost_estimate=pl.CostEstimate(flops=flops, bytes_accessed=moved, transcendentals=0),
        compiler_params=pltpu.CompilerParams(vmem_limit_bytes=16 << 20),
    )(*args)


def swap(block, axis, stride):
    count = lax.axis_size(axis)
    return lax.ppermute(block, axis, [(low, low ^ stride) for low in range(count)])


def own_and_other(part):
    me = lax.axis_index("row")
    return (
        pl.ds(pl.multiple_of(me * part, part), part),
        pl.ds(pl.multiple_of((1 - me) * part, part), part),
    )


def fetch_all(pairs, sems):
    copies = [pltpu.make_async_copy(source, target, sems.at[i]) for i, (source, target) in enumerate(pairs)]
    for copy in copies:
        copy.start()
    return copies


def prepare(
    lower_0h, lower_1h, lower_2h, pattern_h, inv_1h, inv_2h, pack, along,
    lower_0, lower_1, lower_2t, pattern, inv_1, inv_2, sems,
):
    first = 0
    for copy in fetch_all(
        (
            (pattern_h, pattern), (lower_1h, lower_1), (lower_2h, lower_2t), (inv_1h, inv_1), (inv_2h, inv_2),
            (lower_0h, lower_0),
        ),
        sems,
    ):
        copy.wait()
    rows = lower_0.shape[1]
    blocks = pattern.shape[1]
    spread = rows // blocks
    n0, n1 = lower_0.shape[0], lower_1.shape[0]
    part_1, part_2 = lower_1.shape[2], lower_2t.shape[1]
    for b in range(blocks):
        at = pl.ds(b * spread, spread)
        for m in range(n0):
            factor = pattern[0, b, m].astype(BF16)
            pack[pl.ds(first + m * rows + b * spread, spread), :] = lower_0[m, at, :] * factor
        for m in range(n1):
            factor = pattern[0, b, n0 + m].astype(BF16)
            masked = lower_1[m, at, :] * factor
            lanes = pl.ds(m * part_1, part_1)
            pack[pl.ds(first + n0 * rows + b * spread, spread), lanes] = masked
            along[at, lanes] = masked
    lane = lax.broadcasted_iota(jnp.int32, (1, rows), 1) // spread
    keep = jnp.zeros((1, rows), F32)
    for b in range(blocks):
        keep = jnp.where(lane == b, pattern[0, b, n0 + n1].astype(F32), keep)
    short = part_2 // 2
    cut = part_1 // 2
    last = rows + cut + part_2
    for i in range(2):
        masked = (lower_2t[0, pl.ds(i * short, short), :].astype(F32) * keep).astype(BF16)
        pack[pl.ds(first + (n0 + 1) * rows, short), pl.ds(i * rows, rows)] = masked
        along[pl.ds(last, short), pl.ds(i * rows, rows)] = masked
    mine, _ = own_and_other(cut)
    along[pl.ds(rows, cut), :] = inv_1[mine, :]
    along[pl.ds(rows + cut, part_2), :] = inv_2[...]


def leaf_sum(m, row, solved, lower, rhs, keep, send, total):
    leaves = lower.shape[1]
    mine, _ = own_and_other(rhs.shape[2])
    own, other = own_and_other(keep.shape[2])
    acc = dot(lower[row, 0], solved[0])
    for v in range(1, leaves):
        acc = acc + dot(lower[row, v], solved[v])
    total[...] = -acc
    total[mine, :] = total[mine, :] + rhs[row, 0].astype(F32)
    keep[m] = total[:, own]
    send[m] = total[:, other].astype(BF16)


def leaf_a(inverse, right, lower, rhs, solved, keep, send, total):
    for v in range(inverse.shape[0]):
        solved[v] = dot(inverse[v], right[v]).astype(BF16)
    for m in range(keep.shape[0]):
        leaf_sum(m, m, solved, lower, rhs, keep, send, total)


def leaf_b(solved, lower, rhs, keep, send, total):
    late = keep.shape[0]
    for m in range(late):
        leaf_sum(m, lower.shape[0] - late + m, solved, lower, rhs, keep, send, total)


def quarters(half):
    part = half // 2
    bit = lax.rem(lax.axis_index("col"), 2)
    return (
        pl.ds(pl.multiple_of(bit * part, part), part),
        pl.ds(pl.multiple_of((1 - bit) * part, part), part),
    )


def split(total, kept, sent):
    own, other = quarters(total.shape[1])
    kept[...] = total[:, own]
    sent[...] = total[:, other].astype(BF16)


def zero_a(keep, got, pack, pack_o, inverse, solved_out, kept, sent, total):
    size = inverse.shape[1]
    rows = size // 2
    residual = (keep[0] + got[0].astype(F32)).astype(BF16)
    solved = dot(inverse[...], residual).astype(BF16)
    solved_out[...] = solved
    total[...] = keep[1] + got[1].astype(F32)
    for ref, at in zip((pack, pack_o), own_and_other(rows)):
        total[at, :] = total[at, :] - dot(ref[pl.ds(0, rows), :], solved)
    split(total, kept, sent)


def zero_b(keep, got, solved, pack, pack_o, kept_2, sent_2, kept_3, sent_3, total):
    size = solved.shape[0]
    rows = size // 2
    for m, (kept, sent) in enumerate(((kept_2, sent_2), (kept_3, sent_3))):
        total[...] = keep[m] + got[m].astype(F32)
        for ref, at in zip((pack, pack_o), own_and_other(rows)):
            total[at, :] = total[at, :] - dot(ref[pl.ds((m + 1) * rows, rows), :], solved[...])
        split(total, kept, sent)


def one(kept, got, inverse, pack, pack_o, along, along_x, along_xo, solved_own, solved_x, *updates):
    size, part = kept.shape[0], inverse.shape[0]
    rows = size // 2
    first = 3 * rows
    residual = (kept[...] + got[...].astype(F32)).astype(BF16)
    solved_own[...] = dot(inverse[...], residual).astype(BF16)
    cut = part // 2
    for ref, at in zip((along_x, along_xo), own_and_other(cut)):
        solved_x[at, :] = dot(ref[pl.ds(rows, cut), :], residual).astype(BF16)
    own, other = solved_own[...], solved_x[...]
    for m, u in enumerate(updates):
        lanes = pl.ds(m * part, part)
        for ref, ref_x, at in zip((pack, pack_o), (along_x, along_xo), own_and_other(rows)):
            u[at, :] = dot(ref[pl.ds(first, rows), lanes], own) + dot(ref_x[pl.ds(0, rows), lanes], other)


def stack(along, along_x, out):
    part = out.shape[0] // 2
    at = pl.ds(along.shape[0] - part, part)
    out[pl.ds(0, part), :] = along[at, :]
    out[pl.ds(part, part), :] = along_x[at, :]


def difference(kept, got, update, out):
    out[...] = (kept[...] + got[...].astype(F32) - update[...]).astype(BF16)


def two(w2, w2_y, s3, s3_y, pack_o, along, along_x, along_xo, side, side_o, solved_own, v3, to_x):
    size = w2.shape[0]
    rows = size // 2
    part = solved_own.shape[0]
    short = part // 2
    residual = (w2[...].astype(F32) + w2_y[...].astype(F32)).astype(BF16)
    top = along.shape[0] - part - short
    step = part + short
    inverses = ((along, top), (along_x, top), (side, 0), (side, step))
    mine_at = ((along, top + part), (along_x, top + part), (side, part), (side, step + part))
    their_at = (
        (pack_o, pack_o.shape[0] - short), (along_xo, top + part), (side_o, part), (side_o, step + part),
    )
    ranges = own_and_other(rows)
    total = [s3[at, :].astype(F32) + s3_y[at, :].astype(F32) for at in ranges]
    for i, (ref, at) in enumerate(inverses):
        solved = dot(ref[pl.ds(at, part), :], residual).astype(BF16)
        if i == 0:
            solved_own[...] = solved
        if i == 1:
            to_x[pl.ds(size, part), :] = solved
        for j, (low, start) in enumerate((mine_at[i], their_at[i])):
            block = low[pl.ds(start, short), :]
            total[j] = total[j] - dot_t(block[:, :rows], solved[:short]) - dot_t(block[:, rows:], solved[short:])
    for at, value in zip(ranges, total):
        v3[at, :] = value.astype(BF16)
        to_x[at, :] = value.astype(BF16)


def three(v3, v3_z, v3_xz, from_x, inverse, sol1, sol1_x, sol2, out, full):
    size = v3.shape[0]
    own, other = quarters(out.shape[1])
    full[:, own] = (v3[...].astype(F32) + v3_z[...].astype(F32)).astype(BF16)
    full[:, other] = (from_x[pl.ds(0, size), :].astype(F32) + v3_xz[...].astype(F32)).astype(BF16)
    n1, n2 = sol1.shape[0], sol2.shape[0]
    out[pl.ds(0, n1), own] = sol1[...]
    out[pl.ds(0, n1), other] = sol1_x[...]
    out[pl.ds(n1, n2), own] = sol2[...]
    out[pl.ds(n1, n2), other] = from_x[pl.ds(size, n2), :]
    out[pl.ds(n1 + n2, inverse.shape[0]), :] = dot(inverse[...], full[...]).astype(BF16)


def join(own, got, *outs):
    mine, theirs = own_and_other(own.shape[1])
    first = 0
    for out in outs:
        at = pl.ds(first, out.shape[0])
        out[:, mine] = own[at, :]
        out[:, theirs] = got[at, :]
        first += out.shape[0]


PREPARE_FLOPS = 4 * 10**9


def body(
    rhs, leaf_rhs, leaf_inverse, leaf_lower,
    inverse_0, inverse_1, inverse_2, inverse_3,
    lower_0, lower_1, lower_2, sparsity,
):
    levels, _, rows, width = rhs.shape
    leaves, size, _ = leaf_inverse.shape
    half = width // lax.axis_size("row")
    n0 = lower_0.shape[0]
    part_1, part_2 = inverse_1.shape[0], inverse_2.shape[0]
    full = [pltpu.VMEM((size, width), F32)]

    early = 2
    late = levels - early
    short = part_2 // 2
    quarter = half // 2
    square = pltpu.VMEM((size, half), F32)
    kept, sent = ((size, quarter), F32), ((size, quarter), BF16)
    lower_2t, pattern = jnp.swapaxes(lower_2, 1, 2), jnp.transpose(sparsity, (1, 2, 0))
    sources = (lower_0, lower_1, lower_2t, pattern, inverse_1, inverse_2)
    pack, along = call(
        prepare,
        [
            (((n0 + 1) * rows + short, half), BF16),
            ((rows + part_1 // 2 + part_2 + short, half), BF16),
        ],
        *(pltpu.with_memory_space_constraint(x, pltpu.HBM) for x in sources),
        specs=[pl.BlockSpec(memory_space=pltpu.HBM)] * len(sources),
        scratch=[pltpu.VMEM(x.shape, BF16) for x in sources[:3]]
        + [pltpu.SMEM(pattern.shape, jnp.int32)]
        + [pltpu.VMEM(x.shape, BF16) for x in sources[4:]]
        + [pltpu.SemaphoreType.DMA((len(sources),))],
        flops=PREPARE_FLOPS,
    )
    along_x = swap(along, "col", 1)
    solved_leaf, keep_a, send_a = call(
        leaf_a,
        [((leaves, size, width), BF16), ((early, size, half), F32), ((early, size, half), BF16)],
        leaf_inverse, leaf_rhs, leaf_lower, rhs,
        scratch=full, flops=2 * (1 + early) * leaves * size * size * width,
    )
    got_a = swap(send_a, "row", 1)
    pack_o = swap(pack, "row", 1)
    keep_b, send_b = call(
        leaf_b,
        [((late, size, half), F32), ((late, size, half), BF16)],
        solved_leaf, leaf_lower, rhs,
        scratch=full, flops=2 * late * leaves * size * size * width,
    )
    got_b = swap(send_b, "row", 1)
    sol0, kept1, sent1 = call(
        zero_a, [((size, half), BF16), kept, sent],
        keep_a, got_a, pack, pack_o, inverse_0,
        scratch=[square], flops=4 * size * size * half,
    )
    got1 = swap(sent1, "col", 1)
    kept2, sent2, kept3, sent3 = call(
        zero_b, [kept, sent, kept, sent], keep_b, got_b, sol0, pack, pack_o,
        scratch=[square], flops=4 * size * size * half,
    )
    got2 = swap(sent2, "col", 1)
    got3 = swap(sent3, "col", 1)
    along_xo = swap(along_x, "row", 1)
    side = swap(call(stack, [((2 * (part_2 + short), half), BF16)], along, along_x), "col", 2)
    sol1, sol1_for_x, u2, u3 = call(
        one, [((part_1, quarter), BF16)] * 2 + [kept] * 2,
        kept1, got1, inverse_1, pack, pack_o, along, along_x, along_xo,
        flops=6 * size * size * quarter,
    )
    w2 = call(difference, [sent], kept2, got2, u2)
    w2_y = swap(w2, "col", 2)
    sol0_o = swap(sol0, "row", 1)
    side_o = swap(side, "row", 1)
    s3 = call(difference, [sent], kept3, got3, u3)
    s3_y = swap(s3, "col", 2)
    sol1_x = swap(sol1_for_x, "col", 1)
    out0 = call(join, [((size, width), BF16)], sol0, sol0_o)
    sol2, v3, to_x = call(
        two,
        [((part_2, quarter), BF16), sent, ((size + part_2, quarter), BF16)],
        w2, w2_y, s3, s3_y, pack_o, along, along_x, along_xo, side, side_o,
        flops=4 * size * size * quarter,
    )
    v3_xz = swap(v3, "col", 5)
    from_x = swap(to_x, "col", 1)
    v3_z = swap(v3, "col", 4)
    part_3 = inverse_3.shape[0]
    last = call(
        three, [((part_1 + part_2 + part_3, half), BF16)],
        v3, v3_z, v3_xz, from_x, inverse_3, sol1, sol1_x, sol2,
        scratch=[pltpu.VMEM((size, half), BF16)], flops=2 * inverse_3.size * half,
    )
    last_o = swap(last, "row", 1)
    rest = call(join, [((part, width), BF16) for part in (part_1, part_2, part_3)], last, last_o)
    return (out0, *rest)


def solution(mesh):
    return jax.shard_map(
        body,
        mesh=mesh,
        in_specs=(
            P(None, "col", "row", None),
            P(("col", "row"), None, None),
            P(("col", "row"), None, None),
            P(None, ("col", "row"), None, None),
            P("col", None),
            P("col", None),
            P("col", None),
            P("col", None),
            P(None, "row", "col"),
            P(None, "row", "col"),
            P(None, "row", "col"),
            P(None, "col", "row"),
        ),
        out_specs=(P("col", None), P("col", None), P("col", None), P("col", None)),
        check_vma=False,
    )
```

```python
import jax
import jax.numpy as jnp
from jax import lax
from jax.experimental import pallas as pl
from jax.experimental.pallas import tpu as pltpu
from jax.sharding import PartitionSpec as P

F32, BF16 = jnp.float32, jnp.bfloat16
WHOLE = pl.BlockSpec(memory_space=pltpu.VMEM)
SCALARS = pl.BlockSpec(memory_space=pltpu.SMEM)


def dot(a, b):
    return jnp.dot(a, b, preferred_element_type=F32)


def dot_t(a, b):
    return lax.dot_general(a, b, (((0,), (0,)), ((), ())), preferred_element_type=F32)


def call(kernel, outs, *args, scratch=(), flops=0, specs=None):
    outs = [jax.ShapeDtypeStruct(shape, dtype) for shape, dtype in outs]
    moved = sum(a.size * a.dtype.itemsize for a in (*args, *outs))
    single = len(outs) == 1
    return pl.pallas_call(
        kernel,
        out_shape=outs[0] if single else outs,
        in_specs=specs or [WHOLE] * len(args),
        out_specs=WHOLE if single else [WHOLE] * len(outs),
        scratch_shapes=list(scratch),
        cost_estimate=pl.CostEstimate(flops=flops, bytes_accessed=moved, transcendentals=0),
        compiler_params=pltpu.CompilerParams(vmem_limit_bytes=16 << 20),
    )(*args)


def swap(block, axis, stride):
    count = lax.axis_size(axis)
    return lax.ppermute(block, axis, [(low, low ^ stride) for low in range(count)])


def own_and_other(part):
    me = lax.axis_index("row")
    return (
        pl.ds(pl.multiple_of(me * part, part), part),
        pl.ds(pl.multiple_of((1 - me) * part, part), part),
    )


def fetch_all(pairs, sems):
    copies = [pltpu.make_async_copy(source, target, sems.at[i]) for i, (source, target) in enumerate(pairs)]
    for copy in copies:
        copy.start()
    return copies


def prepare(
    lower_0h, lower_1h, lower_2h, pattern_h, inv_1h, inv_2h, pack, along,
    lower_0, lower_1, lower_2t, pattern, inv_1, inv_2, sems,
):
    first = 0
    for copy in fetch_all(
        (
            (pattern_h, pattern), (lower_1h, lower_1), (lower_2h, lower_2t), (inv_1h, inv_1), (inv_2h, inv_2),
            (lower_0h, lower_0),
        ),
        sems,
    ):
        copy.wait()
    rows = lower_0.shape[1]
    blocks = pattern.shape[1]
    spread = rows // blocks
    n0, n1 = lower_0.shape[0], lower_1.shape[0]
    part_1, part_2 = lower_1.shape[2], lower_2t.shape[1]
    for b in range(blocks):
        at = pl.ds(b * spread, spread)
        for m in range(n0):
            factor = pattern[0, b, m].astype(BF16)
            pack[pl.ds(first + m * rows + b * spread, spread), :] = lower_0[m, at, :] * factor
        for m in range(n1):
            factor = pattern[0, b, n0 + m].astype(BF16)
            masked = lower_1[m, at, :] * factor
            lanes = pl.ds(m * part_1, part_1)
            pack[pl.ds(first + n0 * rows + b * spread, spread), lanes] = masked
            along[at, lanes] = masked
    lane = lax.broadcasted_iota(jnp.int32, (1, rows), 1) // spread
    keep = jnp.zeros((1, rows), F32)
    for b in range(blocks):
        keep = jnp.where(lane == b, pattern[0, b, n0 + n1].astype(F32), keep)
    short = part_2 // 2
    cut = part_1 // 2
    last = rows + cut + part_2
    for i in range(2):
        masked = (lower_2t[0, pl.ds(i * short, short), :].astype(F32) * keep).astype(BF16)
        pack[pl.ds(first + (n0 + 1) * rows, short), pl.ds(i * rows, rows)] = masked
        along[pl.ds(last, short), pl.ds(i * rows, rows)] = masked
    mine, _ = own_and_other(cut)
    along[pl.ds(rows, cut), :] = inv_1[mine, :]
    along[pl.ds(rows + cut, part_2), :] = inv_2[...]


def leaf_sum(m, row, solved, lower, rhs, keep, send, total):
    leaves = lower.shape[1]
    mine, _ = own_and_other(rhs.shape[2])
    own, other = own_and_other(keep.shape[2])
    acc = dot(lower[row, 0], solved[0])
    for v in range(1, leaves):
        acc = acc + dot(lower[row, v], solved[v])
    total[...] = -acc
    total[mine, :] = total[mine, :] + rhs[row, 0].astype(F32)
    keep[m] = total[:, own]
    send[m] = total[:, other].astype(BF16)


def leaf_a(inverse, right, lower, rhs, solved, keep, send, total):
    for v in range(inverse.shape[0]):
        solved[v] = dot(inverse[v], right[v]).astype(BF16)
    for m in range(keep.shape[0]):
        leaf_sum(m, m, solved, lower, rhs, keep, send, total)


def leaf_one(m):
    def kernel(solved, lower, rhs, keep, send, total):
        leaf_sum(0, m, solved, lower, rhs, keep, send, total)

    return kernel


def quarters(half):
    part = half // 2
    bit = lax.rem(lax.axis_index("col"), 2)
    return (
        pl.ds(pl.multiple_of(bit * part, part), part),
        pl.ds(pl.multiple_of((1 - bit) * part, part), part),
    )


def split(total, kept, sent):
    own, other = quarters(total.shape[1])
    kept[...] = total[:, own]
    sent[...] = total[:, other].astype(BF16)


def zero_a(keep, got, pack, pack_o, inverse, solved_out, kept, sent, total):
    size = inverse.shape[1]
    rows = size // 2
    residual = (keep[0] + got[0].astype(F32)).astype(BF16)
    solved = dot(inverse[...], residual).astype(BF16)
    solved_out[...] = solved
    total[...] = keep[1] + got[1].astype(F32)
    for ref, at in zip((pack, pack_o), own_and_other(rows)):
        total[at, :] = total[at, :] - dot(ref[pl.ds(0, rows), :], solved)
    split(total, kept, sent)


def zero_next(m):
    def kernel(keep, got, solved, pack, pack_o, kept, sent, total):
        rows = solved.shape[0] // 2
        total[...] = keep[0] + got[0].astype(F32)
        for ref, at in zip((pack, pack_o), own_and_other(rows)):
            total[at, :] = total[at, :] - dot(ref[pl.ds((m - 1) * rows, rows), :], solved[...])
        split(total, kept, sent)

    return kernel


def one(kept, got, inverse, pack, pack_o, along, along_x, along_xo, solved_own, solved_x, *updates):
    size, part = kept.shape[0], inverse.shape[0]
    rows = size // 2
    first = 3 * rows
    residual = (kept[...] + got[...].astype(F32)).astype(BF16)
    solved_own[...] = dot(inverse[...], residual).astype(BF16)
    cut = part // 2
    for ref, at in zip((along_x, along_xo), own_and_other(cut)):
        solved_x[at, :] = dot(ref[pl.ds(rows, cut), :], residual).astype(BF16)
    own, other = solved_own[...], solved_x[...]
    for m, u in enumerate(updates):
        lanes = pl.ds(m * part, part)
        for ref, ref_x, at in zip((pack, pack_o), (along_x, along_xo), own_and_other(rows)):
            u[at, :] = dot(ref[pl.ds(first, rows), lanes], own) + dot(ref_x[pl.ds(0, rows), lanes], other)


def stack(along, along_x, out):
    part = out.shape[0] // 2
    at = pl.ds(along.shape[0] - part, part)
    out[pl.ds(0, part), :] = along[at, :]
    out[pl.ds(part, part), :] = along_x[at, :]


def difference(kept, got, update, out):
    out[...] = (kept[...] + got[...].astype(F32) - update[...]).astype(BF16)


def two(w2, w2_y, pack_o, along, along_x, along_xo, side, side_o, solved_own, solved_x, update):
    size = w2.shape[0]
    rows = size // 2
    part = solved_own.shape[0]
    short = part // 2
    residual = (w2[...].astype(F32) + w2_y[...].astype(F32)).astype(BF16)
    top = along.shape[0] - part - short
    step = part + short
    inverses = ((along, top), (along_x, top), (side, 0), (side, step))
    mine_at = ((along, top + part), (along_x, top + part), (side, part), (side, step + part))
    their_at = (
        (pack_o, pack_o.shape[0] - short), (along_xo, top + part), (side_o, part), (side_o, step + part),
    )
    total = [0.0, 0.0]
    for i, (ref, at) in enumerate(inverses):
        solved = dot(ref[pl.ds(at, part), :], residual).astype(BF16)
        if i < 2:
            (solved_own, solved_x)[i][...] = solved
        for j, (low, start) in enumerate((mine_at[i], their_at[i])):
            block = low[pl.ds(start, short), :]
            total[j] = total[j] + dot_t(block[:, :rows], solved[:short]) + dot_t(block[:, rows:], solved[short:])
    for at, value in zip(own_and_other(rows), total):
        update[at, :] = value


def top_share(s3, s3_y, update, solved_x, v3, to_x):
    size = v3.shape[0]
    value = (s3[...].astype(F32) + s3_y[...].astype(F32) - update[...]).astype(BF16)
    v3[...] = value
    to_x[pl.ds(0, size), :] = value
    to_x[pl.ds(size, solved_x.shape[0]), :] = solved_x[...]


def three(v3, v3_z, v3_xz, from_x, inverse, sol1, sol1_x, sol2, out, full):
    size = v3.shape[0]
    own, other = quarters(out.shape[1])
    full[:, own] = (v3[...].astype(F32) + v3_z[...].astype(F32)).astype(BF16)
    full[:, other] = (from_x[pl.ds(0, size), :].astype(F32) + v3_xz[...].astype(F32)).astype(BF16)
    n1, n2 = sol1.shape[0], sol2.shape[0]
    out[pl.ds(0, n1), own] = sol1[...]
    out[pl.ds(0, n1), other] = sol1_x[...]
    out[pl.ds(n1, n2), own] = sol2[...]
    out[pl.ds(n1, n2), other] = from_x[pl.ds(size, n2), :]
    out[pl.ds(n1 + n2, inverse.shape[0]), :] = dot(inverse[...], full[...]).astype(BF16)


def join(own, got, *outs):
    mine, theirs = own_and_other(own.shape[1])
    first = 0
    for out in outs:
        at = pl.ds(first, out.shape[0])
        out[:, mine] = own[at, :]
        out[:, theirs] = got[at, :]
        first += out.shape[0]


PREPARE_FLOPS = 4 * 10**9


def body(
    rhs, leaf_rhs, leaf_inverse, leaf_lower,
    inverse_0, inverse_1, inverse_2, inverse_3,
    lower_0, lower_1, lower_2, sparsity,
):
    levels, _, rows, width = rhs.shape
    leaves, size, _ = leaf_inverse.shape
    half = width // lax.axis_size("row")
    n0 = lower_0.shape[0]
    part_1, part_2 = inverse_1.shape[0], inverse_2.shape[0]
    full = [pltpu.VMEM((size, width), F32)]

    early = 2
    short = part_2 // 2
    quarter = half // 2
    square = pltpu.VMEM((size, half), F32)
    kept, sent = ((size, quarter), F32), ((size, quarter), BF16)
    lower_2t, pattern = jnp.swapaxes(lower_2, 1, 2), jnp.transpose(sparsity, (1, 2, 0))
    sources = (lower_0, lower_1, lower_2t, pattern, inverse_1, inverse_2)
    pack, along = call(
        prepare,
        [
            (((n0 + 1) * rows + short, half), BF16),
            ((rows + part_1 // 2 + part_2 + short, half), BF16),
        ],
        *(pltpu.with_memory_space_constraint(x, pltpu.HBM) for x in sources),
        specs=[pl.BlockSpec(memory_space=pltpu.HBM)] * len(sources),
        scratch=[pltpu.VMEM(x.shape, BF16) for x in sources[:3]]
        + [pltpu.SMEM(pattern.shape, jnp.int32)]
        + [pltpu.VMEM(x.shape, BF16) for x in sources[4:]]
        + [pltpu.SemaphoreType.DMA((len(sources),))],
        flops=PREPARE_FLOPS,
    )
    along_x = swap(along, "col", 1)
    solved_leaf, keep_a, send_a = call(
        leaf_a,
        [((leaves, size, width), BF16), ((early, size, half), F32), ((early, size, half), BF16)],
        leaf_inverse, leaf_rhs, leaf_lower, rhs,
        scratch=full, flops=2 * (1 + early) * leaves * size * size * width,
    )
    got_a = swap(send_a, "row", 1)
    pack_o = swap(pack, "row", 1)
    kept_m, got_m = {}, {}
    for m in range(early, levels):
        kept_m[m], send_m = call(
            leaf_one(m), [((1, size, half), F32), ((1, size, half), BF16)],
            solved_leaf, leaf_lower, rhs,
            scratch=full, flops=2 * leaves * size * size * width,
        )
        got_m[m] = swap(send_m, "row", 1)
    sol0, kept1, sent1 = call(
        zero_a, [((size, half), BF16), kept, sent],
        keep_a, got_a, pack, pack_o, inverse_0,
        scratch=[square], flops=4 * size * size * half,
    )
    got1 = swap(sent1, "col", 1)
    for m in range(early, levels):
        kept_m[m], sent_m = call(
            zero_next(m), [kept, sent], kept_m[m], got_m[m], sol0, pack, pack_o,
            scratch=[square], flops=2 * size * size * half,
        )
        got_m[m] = swap(sent_m, "col", 1)
    along_xo = swap(along_x, "row", 1)
    side = swap(call(stack, [((2 * (part_2 + short), half), BF16)], along, along_x), "col", 2)
    sol1, sol1_for_x, u2, u3 = call(
        one, [((part_1, quarter), BF16)] * 2 + [kept] * 2,
        kept1, got1, inverse_1, pack, pack_o, along, along_x, along_xo,
        flops=6 * size * size * quarter,
    )
    w2 = call(difference, [sent], kept_m[2], got_m[2], u2)
    w2_y = swap(w2, "col", 2)
    sol0_o = swap(sol0, "row", 1)
    side_o = swap(side, "row", 1)
    s3 = call(difference, [sent], kept_m[3], got_m[3], u3)
    s3_y = swap(s3, "col", 2)
    sol1_x = swap(sol1_for_x, "col", 1)
    out0 = call(join, [((size, width), BF16)], sol0, sol0_o)
    sol2, sol2_for_x, u3_2 = call(
        two, [((part_2, quarter), BF16)] * 2 + [kept],
        w2, w2_y, pack_o, along, along_x, along_xo, side, side_o,
        flops=4 * size * size * quarter,
    )
    v3, to_x = call(top_share, [sent, ((size + part_2, quarter), BF16)], s3, s3_y, u3_2, sol2_for_x)
    v3_xz = swap(v3, "col", 5)
    from_x = swap(to_x, "col", 1)
    v3_z = swap(v3, "col", 4)
    part_3 = inverse_3.shape[0]
    last = call(
        three, [((part_1 + part_2 + part_3, half), BF16)],
        v3, v3_z, v3_xz, from_x, inverse_3, sol1, sol1_x, sol2,
        scratch=[pltpu.VMEM((size, half), BF16)], flops=2 * inverse_3.size * half,
    )
    last_o = swap(last, "row", 1)
    rest = call(join, [((part, width), BF16) for part in (part_1, part_2, part_3)], last, last_o)
    return (out0, *rest)


def solution(mesh):
    return jax.shard_map(
        body,
        mesh=mesh,
        in_specs=(
            P(None, "col", "row", None),
            P(("col", "row"), None, None),
            P(("col", "row"), None, None),
            P(None, ("col", "row"), None, None),
            P("col", None),
            P("col", None),
            P("col", None),
            P("col", None),
            P(None, "row", "col"),
            P(None, "row", "col"),
            P(None, "row", "col"),
            P(None, "col", "row"),
        ),
        out_specs=(P("col", None), P("col", None), P("col", None), P("col", None)),
        check_vma=False,
    )
```

```python
import jax
import jax.numpy as jnp
from jax import lax
from jax.experimental import pallas as pl
from jax.experimental.pallas import tpu as pltpu
from jax.sharding import PartitionSpec as P

F32, BF16 = jnp.float32, jnp.bfloat16
WHOLE = pl.BlockSpec(memory_space=pltpu.VMEM)
SCALARS = pl.BlockSpec(memory_space=pltpu.SMEM)


def dot(a, b):
    return jnp.dot(a, b, preferred_element_type=F32)


def dot_t(a, b):
    return lax.dot_general(a, b, (((0,), (0,)), ((), ())), preferred_element_type=F32)


def call(kernel, outs, *args, scratch=(), flops=0, specs=None):
    outs = [jax.ShapeDtypeStruct(shape, dtype) for shape, dtype in outs]
    moved = sum(a.size * a.dtype.itemsize for a in (*args, *outs))
    single = len(outs) == 1
    return pl.pallas_call(
        kernel,
        out_shape=outs[0] if single else outs,
        in_specs=specs or [WHOLE] * len(args),
        out_specs=WHOLE if single else [WHOLE] * len(outs),
        scratch_shapes=list(scratch),
        cost_estimate=pl.CostEstimate(flops=flops, bytes_accessed=moved, transcendentals=0),
        compiler_params=pltpu.CompilerParams(vmem_limit_bytes=16 << 20),
    )(*args)


def swap(block, axis, stride):
    count = lax.axis_size(axis)
    return lax.ppermute(block, axis, [(low, low ^ stride) for low in range(count)])


def own_and_other(part):
    me = lax.axis_index("row")
    return (
        pl.ds(pl.multiple_of(me * part, part), part),
        pl.ds(pl.multiple_of((1 - me) * part, part), part),
    )


def fetch_all(pairs, sems):
    copies = [pltpu.make_async_copy(source, target, sems.at[i]) for i, (source, target) in enumerate(pairs)]
    for copy in copies:
        copy.start()
    return copies


def prepare(
    lower_0h, lower_1h, lower_2h, pattern_h, inv_1h, inv_2h, pack, along,
    lower_0, lower_1, lower_2t, pattern, inv_1, inv_2, sems,
):
    first = 0
    for copy in fetch_all(
        (
            (pattern_h, pattern), (lower_1h, lower_1), (lower_2h, lower_2t), (inv_1h, inv_1), (inv_2h, inv_2),
            (lower_0h, lower_0),
        ),
        sems,
    ):
        copy.wait()
    rows = lower_0.shape[1]
    blocks = pattern.shape[1]
    spread = rows // blocks
    n0, n1 = lower_0.shape[0], lower_1.shape[0]
    part_1, part_2 = lower_1.shape[2], lower_2t.shape[1]
    for b in range(blocks):
        at = pl.ds(b * spread, spread)
        for m in range(n0):
            factor = pattern[0, b, m].astype(BF16)
            pack[pl.ds(first + m * rows + b * spread, spread), :] = lower_0[m, at, :] * factor
        for m in range(n1):
            factor = pattern[0, b, n0 + m].astype(BF16)
            masked = lower_1[m, at, :] * factor
            lanes = pl.ds(m * part_1, part_1)
            pack[pl.ds(first + n0 * rows + b * spread, spread), lanes] = masked
            along[at, lanes] = masked
    lane = lax.broadcasted_iota(jnp.int32, (1, rows), 1) // spread
    keep = jnp.zeros((1, rows), F32)
    for b in range(blocks):
        keep = jnp.where(lane == b, pattern[0, b, n0 + n1].astype(F32), keep)
    short = part_2 // 2
    cut = part_1 // 2
    last = rows + cut + part_2
    for i in range(2):
        masked = (lower_2t[0, pl.ds(i * short, short), :].astype(F32) * keep).astype(BF16)
        pack[pl.ds(first + (n0 + 1) * rows, short), pl.ds(i * rows, rows)] = masked
        along[pl.ds(last, short), pl.ds(i * rows, rows)] = masked
    mine, _ = own_and_other(cut)
    along[pl.ds(rows, cut), :] = inv_1[mine, :]
    along[pl.ds(rows + cut, part_2), :] = inv_2[...]


def leaf_sum(m, row, solved, lower, rhs, keep, send, total):
    leaves = lower.shape[1]
    mine, _ = own_and_other(rhs.shape[2])
    own, other = own_and_other(keep.shape[2])
    acc = dot(lower[row, 0], solved[0])
    for v in range(1, leaves):
        acc = acc + dot(lower[row, v], solved[v])
    total[...] = -acc
    total[mine, :] = total[mine, :] + rhs[row, 0].astype(F32)
    keep[m] = total[:, own]
    send[m] = total[:, other].astype(BF16)


def leaf_a(inverse, right, lower, rhs, solved, keep, send, total):
    for v in range(inverse.shape[0]):
        solved[v] = dot(inverse[v], right[v]).astype(BF16)
    for m in range(keep.shape[0]):
        leaf_sum(m, m, solved, lower, rhs, keep, send, total)


def leaf_b(solved, lower, rhs, keep, send, total):
    late = keep.shape[0]
    for m in range(late):
        leaf_sum(m, lower.shape[0] - late + m, solved, lower, rhs, keep, send, total)


def quarters(half):
    part = half // 2
    bit = lax.rem(lax.axis_index("col"), 2)
    return (
        pl.ds(pl.multiple_of(bit * part, part), part),
        pl.ds(pl.multiple_of((1 - bit) * part, part), part),
    )


def split(total, kept, sent):
    own, other = quarters(total.shape[1])
    kept[...] = total[:, own]
    sent[...] = total[:, other].astype(BF16)


def zero_a(keep, got, pack, pack_o, inverse, solved_out, kept, sent, total):
    size = inverse.shape[1]
    rows = size // 2
    residual = (keep[0] + got[0].astype(F32)).astype(BF16)
    solved = dot(inverse[...], residual).astype(BF16)
    solved_out[...] = solved
    total[...] = keep[1] + got[1].astype(F32)
    for ref, at in zip((pack, pack_o), own_and_other(rows)):
        total[at, :] = total[at, :] - dot(ref[pl.ds(0, rows), :], solved)
    split(total, kept, sent)


def zero_next(m, row):
    def kernel(keep, got, solved, pack, pack_o, kept, sent, total):
        rows = solved.shape[0] // 2
        total[...] = keep[row] + got[row].astype(F32)
        for ref, at in zip((pack, pack_o), own_and_other(rows)):
            total[at, :] = total[at, :] - dot(ref[pl.ds((m - 1) * rows, rows), :], solved[...])
        split(total, kept, sent)

    return kernel


def one(kept, got, inverse, pack, pack_o, along, along_x, along_xo, solved_own, solved_x, *updates):
    size, part = kept.shape[0], inverse.shape[0]
    rows = size // 2
    first = 3 * rows
    residual = (kept[...] + got[...].astype(F32)).astype(BF16)
    solved_own[...] = dot(inverse[...], residual).astype(BF16)
    cut = part // 2
    for ref, at in zip((along_x, along_xo), own_and_other(cut)):
        solved_x[at, :] = dot(ref[pl.ds(rows, cut), :], residual).astype(BF16)
    own, other = solved_own[...], solved_x[...]
    for m, u in enumerate(updates):
        lanes = pl.ds(m * part, part)
        for ref, ref_x, at in zip((pack, pack_o), (along_x, along_xo), own_and_other(rows)):
            u[at, :] = dot(ref[pl.ds(first, rows), lanes], own) + dot(ref_x[pl.ds(0, rows), lanes], other)


def stack(along, along_x, out):
    part = out.shape[0] // 2
    at = pl.ds(along.shape[0] - part, part)
    out[pl.ds(0, part), :] = along[at, :]
    out[pl.ds(part, part), :] = along_x[at, :]


def difference(kept, got, update, out):
    out[...] = (kept[...] + got[...].astype(F32) - update[...]).astype(BF16)


def two(w2, w2_y, pack_o, along, along_x, along_xo, side, side_o, solved_own, solved_x, update):
    size = w2.shape[0]
    rows = size // 2
    part = solved_own.shape[0]
    short = part // 2
    residual = (w2[...].astype(F32) + w2_y[...].astype(F32)).astype(BF16)
    top = along.shape[0] - part - short
    step = part + short
    inverses = ((along, top), (along_x, top), (side, 0), (side, step))
    mine_at = ((along, top + part), (along_x, top + part), (side, part), (side, step + part))
    their_at = (
        (pack_o, pack_o.shape[0] - short), (along_xo, top + part), (side_o, part), (side_o, step + part),
    )
    total = [0.0, 0.0]
    for i, (ref, at) in enumerate(inverses):
        solved = dot(ref[pl.ds(at, part), :], residual).astype(BF16)
        if i < 2:
            (solved_own, solved_x)[i][...] = solved
        for j, (low, start) in enumerate((mine_at[i], their_at[i])):
            block = low[pl.ds(start, short), :]
            total[j] = total[j] + dot_t(block[:, :rows], solved[:short]) + dot_t(block[:, rows:], solved[short:])
    for at, value in zip(own_and_other(rows), total):
        update[at, :] = value


def top_share(s3, s3_y, update, solved_x, v3, to_x):
    size = v3.shape[0]
    value = (s3[...].astype(F32) + s3_y[...].astype(F32) - update[...]).astype(BF16)
    v3[...] = value
    to_x[pl.ds(0, size), :] = value
    to_x[pl.ds(size, solved_x.shape[0]), :] = solved_x[...]


def half_of(own, got, out):
    mine, theirs = quarters(out.shape[1])
    out[:, mine] = own[...]
    out[:, theirs] = got[...]


def three(v3, v3_z, v3_xz, from_x, inverse, sol2, out, full):
    size = v3.shape[0]
    own, other = quarters(out.shape[1])
    full[:, own] = (v3[...].astype(F32) + v3_z[...].astype(F32)).astype(BF16)
    full[:, other] = (from_x[pl.ds(0, size), :].astype(F32) + v3_xz[...].astype(F32)).astype(BF16)
    part = sol2.shape[0]
    out[pl.ds(0, part), own] = sol2[...]
    out[pl.ds(0, part), other] = from_x[pl.ds(size, part), :]
    out[pl.ds(part, inverse.shape[0]), :] = dot(inverse[...], full[...]).astype(BF16)


def join(own, got, *outs):
    mine, theirs = own_and_other(own.shape[1])
    first = 0
    for out in outs:
        at = pl.ds(first, out.shape[0])
        out[:, mine] = own[at, :]
        out[:, theirs] = got[at, :]
        first += out.shape[0]


PREPARE_FLOPS = 4 * 10**9


def body(
    rhs, leaf_rhs, leaf_inverse, leaf_lower,
    inverse_0, inverse_1, inverse_2, inverse_3,
    lower_0, lower_1, lower_2, sparsity,
):
    levels, _, rows, width = rhs.shape
    leaves, size, _ = leaf_inverse.shape
    half = width // lax.axis_size("row")
    n0 = lower_0.shape[0]
    part_1, part_2 = inverse_1.shape[0], inverse_2.shape[0]
    full = [pltpu.VMEM((size, width), F32)]

    early = 2
    short = part_2 // 2
    quarter = half // 2
    square = pltpu.VMEM((size, half), F32)
    kept, sent = ((size, quarter), F32), ((size, quarter), BF16)
    lower_2t, pattern = jnp.swapaxes(lower_2, 1, 2), jnp.transpose(sparsity, (1, 2, 0))
    sources = (lower_0, lower_1, lower_2t, pattern, inverse_1, inverse_2)
    pack, along = call(
        prepare,
        [
            (((n0 + 1) * rows + short, half), BF16),
            ((rows + part_1 // 2 + part_2 + short, half), BF16),
        ],
        *(pltpu.with_memory_space_constraint(x, pltpu.HBM) for x in sources),
        specs=[pl.BlockSpec(memory_space=pltpu.HBM)] * len(sources),
        scratch=[pltpu.VMEM(x.shape, BF16) for x in sources[:3]]
        + [pltpu.SMEM(pattern.shape, jnp.int32)]
        + [pltpu.VMEM(x.shape, BF16) for x in sources[4:]]
        + [pltpu.SemaphoreType.DMA((len(sources),))],
        flops=PREPARE_FLOPS,
    )
    along_x = swap(along, "col", 1)
    solved_leaf, keep_a, send_a = call(
        leaf_a,
        [((leaves, size, width), BF16), ((early, size, half), F32), ((early, size, half), BF16)],
        leaf_inverse, leaf_rhs, leaf_lower, rhs,
        scratch=full, flops=2 * (1 + early) * leaves * size * size * width,
    )
    got_a = swap(send_a, "row", 1)
    pack_o = swap(pack, "row", 1)
    late = levels - early
    keep_b, send_b = call(
        leaf_b,
        [((late, size, half), F32), ((late, size, half), BF16)],
        solved_leaf, leaf_lower, rhs,
        scratch=full, flops=2 * late * leaves * size * size * width,
    )
    got_b = swap(send_b, "row", 1)
    sol0, kept1, sent1 = call(
        zero_a, [((size, half), BF16), kept, sent],
        keep_a, got_a, pack, pack_o, inverse_0,
        scratch=[square], flops=4 * size * size * half,
    )
    got1 = swap(sent1, "col", 1)
    kept_m, got_m = {}, {}
    for m in range(early, levels):
        kept_m[m], sent_m = call(
            zero_next(m, m - early), [kept, sent], keep_b, got_b, sol0, pack, pack_o,
            scratch=[square], flops=2 * size * size * half,
        )
        got_m[m] = swap(sent_m, "col", 1)
    along_xo = swap(along_x, "row", 1)
    side = swap(call(stack, [((2 * (part_2 + short), half), BF16)], along, along_x), "col", 2)
    sol1, sol1_for_x, u2, u3 = call(
        one, [((part_1, quarter), BF16)] * 2 + [kept] * 2,
        kept1, got1, inverse_1, pack, pack_o, along, along_x, along_xo,
        flops=6 * size * size * quarter,
    )
    w2 = call(difference, [sent], kept_m[2], got_m[2], u2)
    w2_y = swap(w2, "col", 2)
    sol0_o = swap(sol0, "row", 1)
    side_o = swap(side, "row", 1)
    s3 = call(difference, [sent], kept_m[3], got_m[3], u3)
    s3_y = swap(s3, "col", 2)
    sol1_x = swap(sol1_for_x, "col", 1)
    sol1_half = call(half_of, [((part_1, half), BF16)], sol1, sol1_x)
    sol1_o = swap(sol1_half, "row", 1)
    out1 = call(join, [((part_1, width), BF16)], sol1_half, sol1_o)
    out0 = call(join, [((size, width), BF16)], sol0, sol0_o)
    sol2, sol2_for_x, u3_2 = call(
        two, [((part_2, quarter), BF16)] * 2 + [kept],
        w2, w2_y, pack_o, along, along_x, along_xo, side, side_o,
        flops=4 * size * size * quarter,
    )
    v3, to_x = call(top_share, [sent, ((size + part_2, quarter), BF16)], s3, s3_y, u3_2, sol2_for_x)
    v3_xz = swap(v3, "col", 5)
    from_x = swap(to_x, "col", 1)
    v3_z = swap(v3, "col", 4)
    part_3 = inverse_3.shape[0]
    last = call(
        three, [((part_2 + part_3, half), BF16)],
        v3, v3_z, v3_xz, from_x, inverse_3, sol2,
        scratch=[pltpu.VMEM((size, half), BF16)], flops=2 * inverse_3.size * half,
    )
    last_o = swap(last, "row", 1)
    rest = call(join, [((part, width), BF16) for part in (part_2, part_3)], last, last_o)
    return (out0, out1, *rest)


def solution(mesh):
    return jax.shard_map(
        body,
        mesh=mesh,
        in_specs=(
            P(None, "col", "row", None),
            P(("col", "row"), None, None),
            P(("col", "row"), None, None),
            P(None, ("col", "row"), None, None),
            P("col", None),
            P("col", None),
            P("col", None),
            P("col", None),
            P(None, "row", "col"),
            P(None, "row", "col"),
            P(None, "row", "col"),
            P(None, "col", "row"),
        ),
        out_specs=(P("col", None), P("col", None), P("col", None), P("col", None)),
        check_vma=False,
    )
```

```python
import jax
import jax.numpy as jnp
from jax import lax
from jax.experimental import pallas as pl
from jax.experimental.pallas import tpu as pltpu
from jax.sharding import PartitionSpec as P

F32, BF16 = jnp.float32, jnp.bfloat16
WHOLE = pl.BlockSpec(memory_space=pltpu.VMEM)
SCALARS = pl.BlockSpec(memory_space=pltpu.SMEM)


def dot(a, b):
    return jnp.dot(a, b, preferred_element_type=F32)


def call(kernel, outs, *args, scratch=(), flops=0, specs=None):
    outs = [jax.ShapeDtypeStruct(shape, dtype) for shape, dtype in outs]
    moved = sum(a.size * a.dtype.itemsize for a in (*args, *outs))
    single = len(outs) == 1
    return pl.pallas_call(
        kernel,
        out_shape=outs[0] if single else outs,
        in_specs=specs or [WHOLE] * len(args),
        out_specs=WHOLE if single else [WHOLE] * len(outs),
        scratch_shapes=list(scratch),
        cost_estimate=pl.CostEstimate(flops=flops, bytes_accessed=moved, transcendentals=0),
        compiler_params=pltpu.CompilerParams(vmem_limit_bytes=16 << 20),
    )(*args)


def swap(block, axis, stride):
    count = lax.axis_size(axis)
    return lax.ppermute(block, axis, [(low, low ^ stride) for low in range(count)])


def own_and_other(part):
    me = lax.axis_index("row")
    return (
        pl.ds(pl.multiple_of(me * part, part), part),
        pl.ds(pl.multiple_of((1 - me) * part, part), part),
    )


def fetch_all(pairs, sems):
    copies = [pltpu.make_async_copy(source, target, sems.at[i]) for i, (source, target) in enumerate(pairs)]
    for copy in copies:
        copy.start()
    return copies


def prepare(
    lower_0h, lower_1h, lower_2h, pattern_h, inv_1h, inv_2h, inv_3h, pack, along,
    lower_0, lower_1, lower_2t, pattern, inv_1, inv_2, inv_3, sems,
):
    first = 0
    for copy in fetch_all(
        (
            (pattern_h, pattern), (lower_1h, lower_1), (lower_2h, lower_2t), (inv_1h, inv_1), (inv_2h, inv_2),
            (inv_3h, inv_3), (lower_0h, lower_0),
        ),
        sems,
    ):
        copy.wait()
    rows = lower_0.shape[1]
    blocks = pattern.shape[1]
    spread = rows // blocks
    n0, n1 = lower_0.shape[0], lower_1.shape[0]
    part_1, part_2 = lower_1.shape[2], lower_2t.shape[1]
    for b in range(blocks):
        at = pl.ds(b * spread, spread)
        for m in range(n0):
            factor = pattern[0, b, m].astype(BF16)
            pack[pl.ds(first + m * rows + b * spread, spread), :] = lower_0[m, at, :] * factor
        for m in range(n1):
            factor = pattern[0, b, n0 + m].astype(BF16)
            masked = lower_1[m, at, :] * factor
            lanes = pl.ds(m * part_1, part_1)
            pack[pl.ds(first + n0 * rows + b * spread, spread), lanes] = masked
            along[at, lanes] = masked
    lane = lax.broadcasted_iota(jnp.int32, (1, rows), 1) // spread
    keep = jnp.zeros((1, rows), F32)
    for b in range(blocks):
        keep = jnp.where(lane == b, pattern[0, b, n0 + n1].astype(F32), keep)
    short = part_2 // 2
    cut = part_1 // 2
    last = rows + cut + short
    for i in range(2):
        masked = (lower_2t[0, pl.ds(i * short, short), :].astype(F32) * keep).astype(BF16)
        pack[pl.ds(first + (n0 + 1) * rows, short), pl.ds(i * rows, rows)] = masked
        along[pl.ds(last, short), pl.ds(i * rows, rows)] = masked
    mine, _ = own_and_other(cut)
    along[pl.ds(rows, cut), :] = inv_1[mine, :]
    mine, _ = own_and_other(short)
    along[pl.ds(rows + cut, short), :] = inv_2[mine, :]
    along[pl.ds(last + short, inv_3.shape[0]), :] = inv_3[...]


def leaf_sum(m, row, solved, lower, rhs, keep, send, total):
    leaves = lower.shape[1]
    mine, _ = own_and_other(rhs.shape[2])
    own, other = own_and_other(keep.shape[2])
    acc = dot(lower[row, 0], solved[0])
    for v in range(1, leaves):
        acc = acc + dot(lower[row, v], solved[v])
    total[...] = -acc
    total[mine, :] = total[mine, :] + rhs[row, 0].astype(F32)
    keep[m] = total[:, own]
    send[m] = total[:, other].astype(BF16)


def leaf_a(inverse, right, lower, rhs, solved, keep, send, total):
    for v in range(inverse.shape[0]):
        solved[v] = dot(inverse[v], right[v]).astype(BF16)
    for m in range(keep.shape[0]):
        leaf_sum(m, m, solved, lower, rhs, keep, send, total)


def leaf_b(solved, lower, rhs, keep, send, total):
    late = keep.shape[0]
    for m in range(late):
        leaf_sum(m, lower.shape[0] - late + m, solved, lower, rhs, keep, send, total)


def quarters(half):
    part = half // 2
    bit = lax.rem(lax.axis_index("col"), 2)
    return (
        pl.ds(pl.multiple_of(bit * part, part), part),
        pl.ds(pl.multiple_of((1 - bit) * part, part), part),
    )


def split(total, kept, sent):
    own, other = quarters(total.shape[1])
    kept[...] = total[:, own]
    sent[...] = total[:, other].astype(BF16)


def zero_a(keep, got, pack, pack_o, inverse, solved_out, kept, sent, total):
    size = inverse.shape[1]
    rows = size // 2
    residual = (keep[0] + got[0].astype(F32)).astype(BF16)
    solved = dot(inverse[...], residual).astype(BF16)
    solved_out[...] = solved
    total[...] = keep[1] + got[1].astype(F32)
    for ref, at in zip((pack, pack_o), own_and_other(rows)):
        total[at, :] = total[at, :] - dot(ref[pl.ds(0, rows), :], solved)
    split(total, kept, sent)


def zero_next(m, row):
    def kernel(keep, got, solved, pack, pack_o, kept, sent, total):
        rows = solved.shape[0] // 2
        total[...] = keep[row] + got[row].astype(F32)
        for ref, at in zip((pack, pack_o), own_and_other(rows)):
            total[at, :] = total[at, :] - dot(ref[pl.ds((m - 1) * rows, rows), :], solved[...])
        split(total, kept, sent)

    return kernel


def one(kept, got, inverse, pack, pack_o, along, along_x, along_xo, solved_own, solved_x, *updates):
    size, part = kept.shape[0], inverse.shape[0]
    rows = size // 2
    first = 3 * rows
    residual = (kept[...] + got[...].astype(F32)).astype(BF16)
    solved_own[...] = dot(inverse[...], residual).astype(BF16)
    cut = part // 2
    for ref, at in zip((along_x, along_xo), own_and_other(cut)):
        solved_x[at, :] = dot(ref[pl.ds(rows, cut), :], residual).astype(BF16)
    own, other = solved_own[...], solved_x[...]
    for m, u in enumerate(updates):
        lanes = pl.ds(m * part, part)
        for ref, ref_x, at in zip((pack, pack_o), (along_x, along_xo), own_and_other(rows)):
            u[at, :] = dot(ref[pl.ds(first, rows), lanes], own) + dot(ref_x[pl.ds(0, rows), lanes], other)


def stack(along, along_x, out):
    part = out.shape[0] // 2
    rows = along.shape[1] // 2
    at = pl.ds(rows + rows // 2, part)
    out[pl.ds(0, part), :] = along[at, :]
    out[pl.ds(part, part), :] = along_x[at, :]


def difference(kept, got, update, out):
    out[...] = (kept[...] + got[...].astype(F32) - update[...]).astype(BF16)


def whole_2(inverse, along, pack_o, along_x, along_xo, side, side_o, inv_out, low_out, low_t):
    part, size = inverse.shape
    rows, short = size // 2, part // 2
    me = lax.axis_index("row")
    inv_out[pl.ds(0, part), :] = inverse[...]
    first = rows + rows // 2
    halves = [(along_x, along_xo, first), (side, side_o, 0), (side, side_o, part)]
    for i, (mine, theirs, at) in enumerate(halves):
        for ref, which in ((mine, me), (theirs, 1 - me)):
            start = pl.multiple_of((i + 1) * part + which * short, short)
            inv_out[pl.ds(start, short), :] = ref[pl.ds(at, short), :]
    own, other = own_and_other(rows)
    lows = [((along, first + short), (pack_o, pack_o.shape[0] - short))]
    lows += [((mine, at + short), (theirs, at + short)) for mine, theirs, at in halves]
    for i, pair in enumerate(lows):
        for (ref, at), lanes in zip(pair, (own, other)):
            block = ref[pl.ds(at, short), :].astype(F32)
            low_t[pl.ds(i * part, short), lanes] = block[:, :rows]
            low_t[pl.ds(i * part + short, short), lanes] = block[:, rows:]
    low_out[...] = jnp.transpose(low_t[...]).astype(BF16)


def two(w2, w2_y, inverse, low, solved_own, solved_x, update):
    part = solved_own.shape[0]
    residual = (w2[...].astype(F32) + w2_y[...].astype(F32)).astype(BF16)
    solved = dot(inverse[...], residual).astype(BF16)
    solved_own[...] = solved[:part]
    solved_x[...] = solved[part : 2 * part]
    update[...] = dot(low[...], solved)


def top_share(s3, s3_y, update, solved_x, along_x, v3, to_x):
    value = (s3[...].astype(F32) + s3_y[...].astype(F32) - update[...]).astype(BF16)
    v3[...] = value
    part = to_x.shape[0] - solved_x.shape[0]
    to_x[pl.ds(0, part), :] = dot(along_x[pl.ds(along_x.shape[0] - part, part), :], value).astype(BF16)
    to_x[pl.ds(part, solved_x.shape[0]), :] = solved_x[...]


def half_of(own, got, out):
    mine, theirs = quarters(out.shape[1])
    out[:, mine] = own[...]
    out[:, theirs] = got[...]


def three(v3, v3_z, v3_xz, from_x, inverse, sol2, out, full, solved):
    own, other = quarters(out.shape[1])
    full[:, own] = (v3[...].astype(F32) + v3_z[...].astype(F32)).astype(BF16)
    full[:, other] = v3_xz[...]
    part, top = sol2.shape[0], inverse.shape[0]
    solved[...] = dot(inverse[...], full[...])
    solved[:, other] = solved[:, other] + from_x[pl.ds(0, top), :].astype(F32)
    out[pl.ds(0, part), own] = sol2[...]
    out[pl.ds(0, part), other] = from_x[pl.ds(top, part), :]
    out[pl.ds(part, top), :] = solved[...].astype(BF16)


def join(own, got, *outs):
    mine, theirs = own_and_other(own.shape[1])
    first = 0
    for out in outs:
        at = pl.ds(first, out.shape[0])
        out[:, mine] = own[at, :]
        out[:, theirs] = got[at, :]
        first += out.shape[0]


PREPARE_FLOPS = 4 * 10**9


def body(
    rhs, leaf_rhs, leaf_inverse, leaf_lower,
    inverse_0, inverse_1, inverse_2, inverse_3,
    lower_0, lower_1, lower_2, sparsity,
):
    levels, _, rows, width = rhs.shape
    leaves, size, _ = leaf_inverse.shape
    half = width // lax.axis_size("row")
    n0 = lower_0.shape[0]
    part_1, part_2 = inverse_1.shape[0], inverse_2.shape[0]
    full = [pltpu.VMEM((size, width), F32)]

    early = 2
    short = part_2 // 2
    quarter = half // 2
    square = pltpu.VMEM((size, half), F32)
    kept, sent = ((size, quarter), F32), ((size, quarter), BF16)
    lower_2t, pattern = jnp.swapaxes(lower_2, 1, 2), jnp.transpose(sparsity, (1, 2, 0))
    sources = (lower_0, lower_1, lower_2t, pattern, inverse_1, inverse_2, inverse_3)
    part_3 = inverse_3.shape[0]
    pack, along = call(
        prepare,
        [
            (((n0 + 1) * rows + short, half), BF16),
            ((rows + part_1 // 2 + 2 * short + part_3, half), BF16),
        ],
        *(pltpu.with_memory_space_constraint(x, pltpu.HBM) for x in sources),
        specs=[pl.BlockSpec(memory_space=pltpu.HBM)] * len(sources),
        scratch=[pltpu.VMEM(x.shape, BF16) for x in sources[:3]]
        + [pltpu.SMEM(pattern.shape, jnp.int32)]
        + [pltpu.VMEM(x.shape, BF16) for x in sources[4:]]
        + [pltpu.SemaphoreType.DMA((len(sources),))],
        flops=PREPARE_FLOPS,
    )
    along_x = swap(along, "col", 1)
    solved_leaf, keep_a, send_a = call(
        leaf_a,
        [((leaves, size, width), BF16), ((early, size, half), F32), ((early, size, half), BF16)],
        leaf_inverse, leaf_rhs, leaf_lower, rhs,
        scratch=full, flops=2 * (1 + early) * leaves * size * size * width,
    )
    got_a = swap(send_a, "row", 1)
    pack_o = swap(pack, "row", 1)
    late = levels - early
    keep_b, send_b = call(
        leaf_b,
        [((late, size, half), F32), ((late, size, half), BF16)],
        solved_leaf, leaf_lower, rhs,
        scratch=full, flops=2 * late * leaves * size * size * width,
    )
    got_b = swap(send_b, "row", 1)
    sol0, kept1, sent1 = call(
        zero_a, [((size, half), BF16), kept, sent],
        keep_a, got_a, pack, pack_o, inverse_0,
        scratch=[square], flops=4 * size * size * half,
    )
    got1 = swap(sent1, "col", 1)
    kept_m, got_m = {}, {}
    for m in range(early, levels):
        kept_m[m], sent_m = call(
            zero_next(m, m - early), [kept, sent], keep_b, got_b, sol0, pack, pack_o,
            scratch=[square], flops=2 * size * size * half,
        )
        got_m[m] = swap(sent_m, "col", 1)
    along_xo = swap(along_x, "row", 1)
    side = swap(call(stack, [((4 * short, half), BF16)], along, along_x), "col", 2)
    sol1, sol1_for_x, u2, u3 = call(
        one, [((part_1, quarter), BF16)] * 2 + [kept] * 2,
        kept1, got1, inverse_1, pack, pack_o, along, along_x, along_xo,
        flops=6 * size * size * quarter,
    )
    w2 = call(difference, [sent], kept_m[2], got_m[2], u2)
    w2_y = swap(w2, "col", 2)
    sol0_o = swap(sol0, "row", 1)
    side_o = swap(side, "row", 1)
    s3 = call(difference, [sent], kept_m[3], got_m[3], u3)
    s3_y = swap(s3, "col", 2)
    sol1_x = swap(sol1_for_x, "col", 1)
    sol1_half = call(half_of, [((part_1, half), BF16)], sol1, sol1_x)
    sol1_o = swap(sol1_half, "row", 1)
    out1 = call(join, [((part_1, width), BF16)], sol1_half, sol1_o)
    out0 = call(join, [((size, width), BF16)], sol0, sol0_o)
    inv2, low2 = call(
        whole_2, [((size, size), BF16)] * 2,
        inverse_2, along, pack_o, along_x, along_xo, side, side_o, scratch=[pltpu.VMEM((size, size), F32)],
    )
    sol2, sol2_for_x, u3_2 = call(
        two, [((part_2, quarter), BF16)] * 2 + [kept], w2, w2_y, inv2, low2,
        flops=4 * size * size * quarter,
    )
    v3, to_x = call(top_share, [sent, ((part_3 + part_2, quarter), BF16)], s3, s3_y, u3_2, sol2_for_x, along_x)
    v3_xz = swap(v3, "col", 5)
    from_x = swap(to_x, "col", 1)
    v3_z = swap(v3, "col", 4)
    last = call(
        three, [((part_2 + part_3, half), BF16)],
        v3, v3_z, v3_xz, from_x, inverse_3, sol2,
        scratch=[pltpu.VMEM((size, half), BF16), pltpu.VMEM((part_3, half), F32)], flops=2 * inverse_3.size * half,
    )
    last_o = swap(last, "row", 1)
    rest = call(join, [((part, width), BF16) for part in (part_2, part_3)], last, last_o)
    return (out0, out1, *rest)


def solution(mesh):
    return jax.shard_map(
        body,
        mesh=mesh,
        in_specs=(
            P(None, "col", "row", None),
            P(("col", "row"), None, None),
            P(("col", "row"), None, None),
            P(None, ("col", "row"), None, None),
            P("col", None),
            P("col", None),
            P("col", None),
            P("col", None),
            P(None, "row", "col"),
            P(None, "row", "col"),
            P(None, "row", "col"),
            P(None, "col", "row"),
        ),
        out_specs=(P("col", None), P("col", None), P("col", None), P("col", None)),
        check_vma=False,
    )
```

```python
import jax
import jax.numpy as jnp
from jax import lax
from jax.experimental import pallas as pl
from jax.experimental.pallas import tpu as pltpu
from jax.sharding import PartitionSpec as P

F32, BF16 = jnp.float32, jnp.bfloat16
WHOLE = pl.BlockSpec(memory_space=pltpu.VMEM)
SCALARS = pl.BlockSpec(memory_space=pltpu.SMEM)


def dot(a, b):
    return jnp.dot(a, b, preferred_element_type=F32)


def call(kernel, outs, *args, scratch=(), flops=0, specs=None):
    outs = [jax.ShapeDtypeStruct(shape, dtype) for shape, dtype in outs]
    moved = sum(a.size * a.dtype.itemsize for a in (*args, *outs))
    single = len(outs) == 1
    return pl.pallas_call(
        kernel,
        out_shape=outs[0] if single else outs,
        in_specs=specs or [WHOLE] * len(args),
        out_specs=WHOLE if single else [WHOLE] * len(outs),
        scratch_shapes=list(scratch),
        cost_estimate=pl.CostEstimate(flops=flops, bytes_accessed=moved, transcendentals=0),
        compiler_params=pltpu.CompilerParams(vmem_limit_bytes=16 << 20),
    )(*args)


def swap(block, axis, stride):
    count = lax.axis_size(axis)
    return lax.ppermute(block, axis, [(low, low ^ stride) for low in range(count)])


def own_and_other(part):
    me = lax.axis_index("row")
    return (
        pl.ds(pl.multiple_of(me * part, part), part),
        pl.ds(pl.multiple_of((1 - me) * part, part), part),
    )


def fetch_all(pairs, sems):
    copies = [pltpu.make_async_copy(source, target, sems.at[i]) for i, (source, target) in enumerate(pairs)]
    for copy in copies:
        copy.start()
    return copies


def prepare(
    lower_0h, lower_1h, lower_2h, pattern_h, inv_1h, inv_2h, inv_3h, pack, along,
    lower_0, lower_1, lower_2t, pattern, inv_1, inv_2, inv_3, sems,
):
    first = 0
    for copy in fetch_all(
        (
            (pattern_h, pattern), (lower_1h, lower_1), (lower_2h, lower_2t), (inv_1h, inv_1), (inv_2h, inv_2),
            (inv_3h, inv_3), (lower_0h, lower_0),
        ),
        sems,
    ):
        copy.wait()
    rows = lower_0.shape[1]
    blocks = pattern.shape[1]
    spread = rows // blocks
    n0, n1 = lower_0.shape[0], lower_1.shape[0]
    part_1, part_2 = lower_1.shape[2], lower_2t.shape[1]
    for b in range(blocks):
        at = pl.ds(b * spread, spread)
        for m in range(n0):
            factor = pattern[0, b, m].astype(BF16)
            pack[pl.ds(first + m * rows + b * spread, spread), :] = lower_0[m, at, :] * factor
        for m in range(n1):
            factor = pattern[0, b, n0 + m].astype(BF16)
            masked = lower_1[m, at, :] * factor
            lanes = pl.ds(m * part_1, part_1)
            pack[pl.ds(first + n0 * rows + b * spread, spread), lanes] = masked
            along[at, lanes] = masked
    lane = lax.broadcasted_iota(jnp.int32, (1, rows), 1) // spread
    keep = jnp.zeros((1, rows), F32)
    for b in range(blocks):
        keep = jnp.where(lane == b, pattern[0, b, n0 + n1].astype(F32), keep)
    short = part_2 // 2
    cut = part_1 // 2
    last = rows + cut + short
    for i in range(2):
        masked = (lower_2t[0, pl.ds(i * short, short), :].astype(F32) * keep).astype(BF16)
        pack[pl.ds(first + (n0 + 1) * rows, short), pl.ds(i * rows, rows)] = masked
        along[pl.ds(last, short), pl.ds(i * rows, rows)] = masked
    mine, _ = own_and_other(cut)
    along[pl.ds(rows, cut), :] = inv_1[mine, :]
    mine, _ = own_and_other(short)
    along[pl.ds(rows + cut, short), :] = inv_2[mine, :]
    along[pl.ds(last + short, inv_3.shape[0]), :] = inv_3[...]


def leaf_sum(m, row, solved, lower, rhs, keep, send):
    leaves, size = lower.shape[1], lower.shape[2]
    rows = rhs.shape[2]
    first = lax.axis_index("row") == 0
    own, other = own_and_other(keep.shape[2])
    for lanes, out in ((other, send), (own, keep)):
        acc = dot(lower[row, 0], solved[0, :, lanes])
        for v in range(1, leaves):
            acc = acc + dot(lower[row, v], solved[v, :, lanes])
        piece = rhs[row, 0, :, lanes].astype(F32)
        none = jnp.zeros_like(piece)
        out[m, pl.ds(0, rows), :] = (jnp.where(first, piece, none) - acc[:rows]).astype(out.dtype)
        out[m, pl.ds(rows, size - rows), :] = (jnp.where(first, none, piece) - acc[rows:]).astype(out.dtype)


def leaf_a(inverse, right, lower, rhs, solved, keep, send):
    for v in range(inverse.shape[0]):
        solved[v] = dot(inverse[v], right[v]).astype(BF16)
    for m in range(keep.shape[0]):
        leaf_sum(m, m, solved, lower, rhs, keep, send)


def leaf_b(solved, lower, rhs, keep, send):
    late = keep.shape[0]
    for m in range(late):
        leaf_sum(m, lower.shape[0] - late + m, solved, lower, rhs, keep, send)


def quarters(half):
    part = half // 2
    bit = lax.rem(lax.axis_index("col"), 2)
    return (
        pl.ds(pl.multiple_of(bit * part, part), part),
        pl.ds(pl.multiple_of((1 - bit) * part, part), part),
    )


def split(total, kept, sent):
    part = kept.shape[1]
    low, high = total[:, :part], total[:, part:]
    first = lax.rem(lax.axis_index("col"), 2) == 0
    kept[...] = jnp.where(first, low, high)
    sent[...] = jnp.where(first, high, low).astype(BF16)


def lower_block(pack, pack_o, m, rows):
    at = pl.ds(m * rows, rows)
    mine, theirs = pack[at, :], pack_o[at, :]
    first = lax.axis_index("row") == 0
    return jnp.concatenate([jnp.where(first, mine, theirs), jnp.where(first, theirs, mine)], axis=0)


def zero_a(keep, got, pack, pack_o, inverse, solved_out, kept, sent):
    residual = (keep[0] + got[0].astype(F32)).astype(BF16)
    solved = dot(inverse[...], residual).astype(BF16)
    solved_out[...] = solved
    low = lower_block(pack, pack_o, 0, inverse.shape[1] // 2)
    split(keep[1] + got[1].astype(F32) - dot(low, solved), kept, sent)


def zero_next(m, row):
    def kernel(keep, got, solved, pack, pack_o, kept, sent):
        low = lower_block(pack, pack_o, m - 1, solved.shape[0] // 2)
        split(keep[row] + got[row].astype(F32) - dot(low, solved[...]), kept, sent)

    return kernel


def one(kept, got, inverse, pack, pack_o, along, along_x, along_xo, solved_own, solved_x, *updates):
    size, part = kept.shape[0], inverse.shape[0]
    rows = size // 2
    first = 3 * rows
    residual = (kept[...] + got[...].astype(F32)).astype(BF16)
    solved_own[...] = dot(inverse[...], residual).astype(BF16)
    cut = part // 2
    for ref, at in zip((along_x, along_xo), own_and_other(cut)):
        solved_x[at, :] = dot(ref[pl.ds(rows, cut), :], residual).astype(BF16)
    own, other = solved_own[...], solved_x[...]
    for m, u in enumerate(updates):
        lanes = pl.ds(m * part, part)
        for ref, ref_x, at in zip((pack, pack_o), (along_x, along_xo), own_and_other(rows)):
            u[at, :] = dot(ref[pl.ds(first, rows), lanes], own) + dot(ref_x[pl.ds(0, rows), lanes], other)


def stack(along, along_x, out):
    part = out.shape[0] // 2
    rows = along.shape[1] // 2
    at = pl.ds(rows + rows // 2, part)
    out[pl.ds(0, part), :] = along[at, :]
    out[pl.ds(part, part), :] = along_x[at, :]


def difference(kept, got, update, out):
    out[...] = (kept[...] + got[...].astype(F32) - update[...]).astype(BF16)


def whole_2(inverse, along, pack_o, along_x, along_xo, side, side_o, inv_out, low_out, low_t):
    part, size = inverse.shape
    rows, short = size // 2, part // 2
    me = lax.axis_index("row")
    inv_out[pl.ds(0, part), :] = inverse[...]
    first = rows + rows // 2
    halves = [(along_x, along_xo, first), (side, side_o, 0), (side, side_o, part)]
    for i, (mine, theirs, at) in enumerate(halves):
        for ref, which in ((mine, me), (theirs, 1 - me)):
            start = pl.multiple_of((i + 1) * part + which * short, short)
            inv_out[pl.ds(start, short), :] = ref[pl.ds(at, short), :]
    own, other = own_and_other(rows)
    lows = [((along, first + short), (pack_o, pack_o.shape[0] - short))]
    lows += [((mine, at + short), (theirs, at + short)) for mine, theirs, at in halves]
    for i, pair in enumerate(lows):
        for (ref, at), lanes in zip(pair, (own, other)):
            block = ref[pl.ds(at, short), :].astype(F32)
            low_t[pl.ds(i * part, short), lanes] = block[:, :rows]
            low_t[pl.ds(i * part + short, short), lanes] = block[:, rows:]
    low_out[...] = jnp.transpose(low_t[...]).astype(BF16)


def two(w2, w2_y, inverse, low, solved_own, solved_x, update):
    part = solved_own.shape[0]
    residual = (w2[...].astype(F32) + w2_y[...].astype(F32)).astype(BF16)
    solved = dot(inverse[...], residual).astype(BF16)
    solved_own[...] = solved[:part]
    solved_x[...] = solved[part : 2 * part]
    update[...] = dot(low[...], solved)


def top_share(s3, s3_y, update, solved_x, along_x, v3, to_x):
    value = (s3[...].astype(F32) + s3_y[...].astype(F32) - update[...]).astype(BF16)
    v3[...] = value
    part = to_x.shape[0] - solved_x.shape[0]
    to_x[pl.ds(0, part), :] = dot(along_x[pl.ds(along_x.shape[0] - part, part), :], value).astype(BF16)
    to_x[pl.ds(part, solved_x.shape[0]), :] = solved_x[...]


def half_of(own, got, out):
    mine, theirs = quarters(out.shape[1])
    out[:, mine] = own[...]
    out[:, theirs] = got[...]


def three(v3, v3_z, v3_xz, from_x, inverse, sol2, out, full, solved):
    own, other = quarters(out.shape[1])
    full[:, own] = (v3[...].astype(F32) + v3_z[...].astype(F32)).astype(BF16)
    full[:, other] = v3_xz[...]
    part, top = sol2.shape[0], inverse.shape[0]
    solved[...] = dot(inverse[...], full[...])
    solved[:, other] = solved[:, other] + from_x[pl.ds(0, top), :].astype(F32)
    out[pl.ds(0, part), own] = sol2[...]
    out[pl.ds(0, part), other] = from_x[pl.ds(top, part), :]
    out[pl.ds(part, top), :] = solved[...].astype(BF16)


def join(own, got, *outs):
    mine, theirs = own_and_other(own.shape[1])
    first = 0
    for out in outs:
        at = pl.ds(first, out.shape[0])
        out[:, mine] = own[at, :]
        out[:, theirs] = got[at, :]
        first += out.shape[0]


PREPARE_FLOPS = 4 * 10**9


def body(
    rhs, leaf_rhs, leaf_inverse, leaf_lower,
    inverse_0, inverse_1, inverse_2, inverse_3,
    lower_0, lower_1, lower_2, sparsity,
):
    levels, _, rows, width = rhs.shape
    leaves, size, _ = leaf_inverse.shape
    half = width // lax.axis_size("row")
    n0 = lower_0.shape[0]
    part_1, part_2 = inverse_1.shape[0], inverse_2.shape[0]

    early = 2
    short = part_2 // 2
    quarter = half // 2
    kept, sent = ((size, quarter), F32), ((size, quarter), BF16)
    lower_2t, pattern = jnp.swapaxes(lower_2, 1, 2), jnp.transpose(sparsity, (1, 2, 0))
    sources = (lower_0, lower_1, lower_2t, pattern, inverse_1, inverse_2, inverse_3)
    part_3 = inverse_3.shape[0]
    pack, along = call(
        prepare,
        [
            (((n0 + 1) * rows + short, half), BF16),
            ((rows + part_1 // 2 + 2 * short + part_3, half), BF16),
        ],
        *(pltpu.with_memory_space_constraint(x, pltpu.HBM) for x in sources),
        specs=[pl.BlockSpec(memory_space=pltpu.HBM)] * len(sources),
        scratch=[pltpu.VMEM(x.shape, BF16) for x in sources[:3]]
        + [pltpu.SMEM(pattern.shape, jnp.int32)]
        + [pltpu.VMEM(x.shape, BF16) for x in sources[4:]]
        + [pltpu.SemaphoreType.DMA((len(sources),))],
        flops=PREPARE_FLOPS,
    )
    along_x = swap(along, "col", 1)
    solved_leaf, keep_a, send_a = call(
        leaf_a,
        [((leaves, size, width), BF16), ((early, size, half), F32), ((early, size, half), BF16)],
        leaf_inverse, leaf_rhs, leaf_lower, rhs,
        flops=2 * (1 + early) * leaves * size * size * width,
    )
    got_a = swap(send_a, "row", 1)
    pack_o = swap(pack, "row", 1)
    late = levels - early
    keep_b, send_b = call(
        leaf_b,
        [((late, size, half), F32), ((late, size, half), BF16)],
        solved_leaf, leaf_lower, rhs,
        flops=2 * late * leaves * size * size * width,
    )
    got_b = swap(send_b, "row", 1)
    sol0, kept1, sent1 = call(
        zero_a, [((size, half), BF16), kept, sent],
        keep_a, got_a, pack, pack_o, inverse_0,
        flops=4 * size * size * half,
    )
    got1 = swap(sent1, "col", 1)
    kept_m, got_m = {}, {}
    for m in range(early, levels):
        kept_m[m], sent_m = call(
            zero_next(m, m - early), [kept, sent], keep_b, got_b, sol0, pack, pack_o,
            flops=2 * size * size * half,
        )
        got_m[m] = swap(sent_m, "col", 1)
    along_xo = swap(along_x, "row", 1)
    side = swap(call(stack, [((4 * short, half), BF16)], along, along_x), "col", 2)
    sol1, sol1_for_x, u2, u3 = call(
        one, [((part_1, quarter), BF16)] * 2 + [kept] * 2,
        kept1, got1, inverse_1, pack, pack_o, along, along_x, along_xo,
        flops=6 * size * size * quarter,
    )
    w2 = call(difference, [sent], kept_m[2], got_m[2], u2)
    w2_y = swap(w2, "col", 2)
    sol0_o = swap(sol0, "row", 1)
    side_o = swap(side, "row", 1)
    s3 = call(difference, [sent], kept_m[3], got_m[3], u3)
    s3_y = swap(s3, "col", 2)
    sol1_x = swap(sol1_for_x, "col", 1)
    sol1_half = call(half_of, [((part_1, half), BF16)], sol1, sol1_x)
    sol1_o = swap(sol1_half, "row", 1)
    out1 = call(join, [((part_1, width), BF16)], sol1_half, sol1_o)
    out0 = call(join, [((size, width), BF16)], sol0, sol0_o)
    inv2, low2 = call(
        whole_2, [((size, size), BF16)] * 2,
        inverse_2, along, pack_o, along_x, along_xo, side, side_o, scratch=[pltpu.VMEM((size, size), F32)],
    )
    sol2, sol2_for_x, u3_2 = call(
        two, [((part_2, quarter), BF16)] * 2 + [kept], w2, w2_y, inv2, low2,
        flops=4 * size * size * quarter,
    )
    v3, to_x = call(top_share, [sent, ((part_3 + part_2, quarter), BF16)], s3, s3_y, u3_2, sol2_for_x, along_x)
    v3_xz = swap(v3, "col", 5)
    from_x = swap(to_x, "col", 1)
    v3_z = swap(v3, "col", 4)
    last = call(
        three, [((part_2 + part_3, half), BF16)],
        v3, v3_z, v3_xz, from_x, inverse_3, sol2,
        scratch=[pltpu.VMEM((size, half), BF16), pltpu.VMEM((part_3, half), F32)], flops=2 * inverse_3.size * half,
    )
    last_o = swap(last, "row", 1)
    rest = call(join, [((part, width), BF16) for part in (part_2, part_3)], last, last_o)
    return (out0, out1, *rest)


def solution(mesh):
    return jax.shard_map(
        body,
        mesh=mesh,
        in_specs=(
            P(None, "col", "row", None),
            P(("col", "row"), None, None),
            P(("col", "row"), None, None),
            P(None, ("col", "row"), None, None),
            P("col", None),
            P("col", None),
            P("col", None),
            P("col", None),
            P(None, "row", "col"),
            P(None, "row", "col"),
            P(None, "row", "col"),
            P(None, "col", "row"),
        ),
        out_specs=(P("col", None), P("col", None), P("col", None), P("col", None)),
        check_vma=False,
    )
```

```python
import jax
import jax.numpy as jnp
from jax import lax
from jax.experimental import pallas as pl
from jax.experimental.pallas import tpu as pltpu
from jax.sharding import PartitionSpec as P

F32, BF16 = jnp.float32, jnp.bfloat16
WHOLE = pl.BlockSpec(memory_space=pltpu.VMEM)
SCALARS = pl.BlockSpec(memory_space=pltpu.SMEM)


def dot(a, b):
    return jnp.dot(a, b, preferred_element_type=F32)


def call(kernel, outs, *args, scratch=(), flops=0, specs=None):
    outs = [jax.ShapeDtypeStruct(shape, dtype) for shape, dtype in outs]
    moved = sum(a.size * a.dtype.itemsize for a in (*args, *outs))
    single = len(outs) == 1
    return pl.pallas_call(
        kernel,
        out_shape=outs[0] if single else outs,
        in_specs=specs or [WHOLE] * len(args),
        out_specs=WHOLE if single else [WHOLE] * len(outs),
        scratch_shapes=list(scratch),
        cost_estimate=pl.CostEstimate(flops=flops, bytes_accessed=moved, transcendentals=0),
        compiler_params=pltpu.CompilerParams(vmem_limit_bytes=16 << 20),
    )(*args)


def swap(block, axis, stride):
    count = lax.axis_size(axis)
    return lax.ppermute(block, axis, [(low, low ^ stride) for low in range(count)])


def own_and_other(part):
    me = lax.axis_index("row")
    return (
        pl.ds(pl.multiple_of(me * part, part), part),
        pl.ds(pl.multiple_of((1 - me) * part, part), part),
    )


def fetch_all(pairs, sems):
    copies = [pltpu.make_async_copy(source, target, sems.at[i]) for i, (source, target) in enumerate(pairs)]
    for copy in copies:
        copy.start()
    return copies


def prepare(
    lower_0h, lower_1h, lower_2h, pattern_h, inv_1h, inv_2h, inv_3h, pack, along,
    lower_0, lower_1, lower_2t, pattern, inv_1, inv_2, inv_3, sems,
):
    first = 0
    for copy in fetch_all(
        (
            (pattern_h, pattern), (lower_1h, lower_1), (lower_2h, lower_2t), (inv_1h, inv_1), (inv_2h, inv_2),
            (inv_3h, inv_3), (lower_0h, lower_0),
        ),
        sems,
    ):
        copy.wait()
    rows = lower_0.shape[1]
    blocks = pattern.shape[1]
    spread = rows // blocks
    n0, n1 = lower_0.shape[0], lower_1.shape[0]
    part_1, part_2 = lower_1.shape[2], lower_2t.shape[1]
    for b in range(blocks):
        at = pl.ds(b * spread, spread)
        for m in range(n0):
            factor = pattern[0, b, m].astype(BF16)
            pack[pl.ds(first + m * rows + b * spread, spread), :] = lower_0[m, at, :] * factor
        for m in range(n1):
            factor = pattern[0, b, n0 + m].astype(BF16)
            masked = lower_1[m, at, :] * factor
            lanes = pl.ds(m * part_1, part_1)
            pack[pl.ds(first + n0 * rows + b * spread, spread), lanes] = masked
            along[at, lanes] = masked
    lane = lax.broadcasted_iota(jnp.int32, (1, rows), 1) // spread
    keep = jnp.zeros((1, rows), F32)
    for b in range(blocks):
        keep = jnp.where(lane == b, pattern[0, b, n0 + n1].astype(F32), keep)
    short = part_2 // 2
    cut = part_1 // 2
    last = rows + cut + short
    for i in range(2):
        masked = (lower_2t[0, pl.ds(i * short, short), :].astype(F32) * keep).astype(BF16)
        pack[pl.ds(first + (n0 + 1) * rows, short), pl.ds(i * rows, rows)] = masked
        along[pl.ds(last, short), pl.ds(i * rows, rows)] = masked
    mine, _ = own_and_other(cut)
    along[pl.ds(rows, cut), :] = inv_1[mine, :]
    mine, _ = own_and_other(short)
    along[pl.ds(rows + cut, short), :] = inv_2[mine, :]
    along[pl.ds(last + short, inv_3.shape[0]), :] = inv_3[...]


def leaf_sum(m, row, solved, lower, rhs, keep, send):
    leaves, size = lower.shape[1], lower.shape[2]
    rows = rhs.shape[2]
    first = lax.axis_index("row") == 0
    own, other = own_and_other(keep.shape[2])
    for lanes, out in ((other, send), (own, keep)):
        acc = dot(lower[row, 0], solved[0, :, lanes])
        for v in range(1, leaves):
            acc = acc + dot(lower[row, v], solved[v, :, lanes])
        piece = rhs[row, 0, :, lanes].astype(F32)
        none = jnp.zeros_like(piece)
        out[m, pl.ds(0, rows), :] = (jnp.where(first, piece, none) - acc[:rows]).astype(out.dtype)
        out[m, pl.ds(rows, size - rows), :] = (jnp.where(first, none, piece) - acc[rows:]).astype(out.dtype)


def leaf_a(inverse, right, lower, rhs, solved, keep, send):
    for v in range(inverse.shape[0]):
        solved[v] = dot(inverse[v], right[v]).astype(BF16)
    for m in range(keep.shape[0]):
        leaf_sum(m, m, solved, lower, rhs, keep, send)


def leaf_b(solved, lower, rhs, keep, send):
    late = keep.shape[0]
    for m in range(late):
        leaf_sum(m, lower.shape[0] - late + m, solved, lower, rhs, keep, send)


def quarters(half):
    part = half // 2
    bit = lax.rem(lax.axis_index("col"), 2)
    return (
        pl.ds(pl.multiple_of(bit * part, part), part),
        pl.ds(pl.multiple_of((1 - bit) * part, part), part),
    )


def split(total, kept, sent):
    part = kept.shape[1]
    low, high = total[:, :part], total[:, part:]
    first = lax.rem(lax.axis_index("col"), 2) == 0
    kept[...] = jnp.where(first, low, high)
    sent[...] = jnp.where(first, high, low).astype(BF16)


def lower_block(pack, pack_o, m, rows):
    at = pl.ds(m * rows, rows)
    mine, theirs = pack[at, :], pack_o[at, :]
    first = lax.axis_index("row") == 0
    return jnp.concatenate([jnp.where(first, mine, theirs), jnp.where(first, theirs, mine)], axis=0)


def zero_a(keep, got, pack, pack_o, inverse, solved_out, kept, sent):
    residual = (keep[0] + got[0].astype(F32)).astype(BF16)
    solved = dot(inverse[...], residual).astype(BF16)
    solved_out[...] = solved
    low = lower_block(pack, pack_o, 0, inverse.shape[1] // 2)
    split(keep[1] + got[1].astype(F32) - dot(low, solved), kept, sent)


def zero_next(m, row):
    def kernel(keep, got, solved, pack, pack_o, kept, sent):
        low = lower_block(pack, pack_o, m - 1, solved.shape[0] // 2)
        split(keep[row] + got[row].astype(F32) - dot(low, solved[...]), kept, sent)

    return kernel


def one(kept, got, inverse, pack, pack_o, along, along_x, along_xo, solved_own, solved_x, *updates):
    size, part = kept.shape[0], inverse.shape[0]
    rows = size // 2
    first = 3 * rows
    residual = (kept[...] + got[...].astype(F32)).astype(BF16)
    solved_own[...] = dot(inverse[...], residual).astype(BF16)
    cut = part // 2
    for ref, at in zip((along_x, along_xo), own_and_other(cut)):
        solved_x[at, :] = dot(ref[pl.ds(rows, cut), :], residual).astype(BF16)
    own, other = solved_own[...], solved_x[...]
    for m, u in enumerate(updates):
        lanes = pl.ds(m * part, part)
        for ref, ref_x, at in zip((pack, pack_o), (along_x, along_xo), own_and_other(rows)):
            u[at, :] = dot(ref[pl.ds(first, rows), lanes], own) + dot(ref_x[pl.ds(0, rows), lanes], other)


def stack(along, along_x, out):
    part = out.shape[0] // 2
    rows = along.shape[1] // 2
    at = pl.ds(rows + rows // 2, part)
    out[pl.ds(0, part), :] = along[at, :]
    out[pl.ds(part, part), :] = along_x[at, :]


def difference(kept, got, update, out):
    out[...] = (kept[...] + got[...].astype(F32) - update[...]).astype(BF16)


def whole_2(inverse, along, pack_o, along_x, along_xo, side, side_o, inv_out, low_out, low_t):
    part, size = inverse.shape
    rows, short = size // 2, part // 2
    me = lax.axis_index("row")
    inv_out[pl.ds(0, part), :] = inverse[...]
    first = rows + rows // 2
    halves = [(along_x, along_xo, first), (side, side_o, 0), (side, side_o, part)]
    for i, (mine, theirs, at) in enumerate(halves):
        for ref, which in ((mine, me), (theirs, 1 - me)):
            start = pl.multiple_of((i + 1) * part + which * short, short)
            inv_out[pl.ds(start, short), :] = ref[pl.ds(at, short), :]
    own, other = own_and_other(rows)
    lows = [((along, first + short), (pack_o, pack_o.shape[0] - short))]
    lows += [((mine, at + short), (theirs, at + short)) for mine, theirs, at in halves]
    for i, pair in enumerate(lows):
        for (ref, at), lanes in zip(pair, (own, other)):
            block = ref[pl.ds(at, short), :].astype(F32)
            low_t[pl.ds(i * part, short), lanes] = block[:, :rows]
            low_t[pl.ds(i * part + short, short), lanes] = block[:, rows:]
    low_out[...] = jnp.transpose(low_t[...]).astype(BF16)


def two(w2, w2_y, inverse, low, solved_own, solved_x, update):
    part = solved_own.shape[0]
    residual = (w2[...].astype(F32) + w2_y[...].astype(F32)).astype(BF16)
    solved = dot(inverse[...], residual).astype(BF16)
    solved_own[...] = solved[:part]
    solved_x[...] = solved[part : 2 * part]
    update[...] = dot(low[...], solved)


def top_share(s3, s3_y, update, solved_x, along_x, v3, to_x):
    value = (s3[...].astype(F32) + s3_y[...].astype(F32) - update[...]).astype(BF16)
    v3[...] = value
    part = to_x.shape[0] - solved_x.shape[0]
    to_x[pl.ds(0, part), :] = dot(along_x[pl.ds(along_x.shape[0] - part, part), :], value).astype(BF16)
    to_x[pl.ds(part, solved_x.shape[0]), :] = solved_x[...]


def half_of(own, got, out):
    mine, theirs = quarters(out.shape[1])
    out[:, mine] = own[...]
    out[:, theirs] = got[...]


def three(v3, v3_z, v3_xz, inverse, solved, full):
    own, other = quarters(solved.shape[1])
    full[:, own] = (v3[...].astype(F32) + v3_z[...].astype(F32)).astype(BF16)
    full[:, other] = v3_xz[...]
    solved[...] = dot(inverse[...], full[...])


def lay(solved, from_x, sol2, out):
    own, other = quarters(out.shape[1])
    part, top = sol2.shape[0], solved.shape[0]
    out[pl.ds(0, part), own] = sol2[...]
    out[pl.ds(0, part), other] = from_x[pl.ds(top, part), :]
    low = pl.ds(part, top)
    out[low, own] = solved[:, own].astype(BF16)
    out[low, other] = (solved[:, other] + from_x[pl.ds(0, top), :].astype(F32)).astype(BF16)


def join(own, got, *outs):
    mine, theirs = own_and_other(own.shape[1])
    first = 0
    for out in outs:
        at = pl.ds(first, out.shape[0])
        out[:, mine] = own[at, :]
        out[:, theirs] = got[at, :]
        first += out.shape[0]


PREPARE_FLOPS = 4 * 10**9


def body(
    rhs, leaf_rhs, leaf_inverse, leaf_lower,
    inverse_0, inverse_1, inverse_2, inverse_3,
    lower_0, lower_1, lower_2, sparsity,
):
    levels, _, rows, width = rhs.shape
    leaves, size, _ = leaf_inverse.shape
    half = width // lax.axis_size("row")
    n0 = lower_0.shape[0]
    part_1, part_2 = inverse_1.shape[0], inverse_2.shape[0]

    early = 2
    short = part_2 // 2
    quarter = half // 2
    kept, sent = ((size, quarter), F32), ((size, quarter), BF16)
    lower_2t, pattern = jnp.swapaxes(lower_2, 1, 2), jnp.transpose(sparsity, (1, 2, 0))
    sources = (lower_0, lower_1, lower_2t, pattern, inverse_1, inverse_2, inverse_3)
    part_3 = inverse_3.shape[0]
    pack, along = call(
        prepare,
        [
            (((n0 + 1) * rows + short, half), BF16),
            ((rows + part_1 // 2 + 2 * short + part_3, half), BF16),
        ],
        *(pltpu.with_memory_space_constraint(x, pltpu.HBM) for x in sources),
        specs=[pl.BlockSpec(memory_space=pltpu.HBM)] * len(sources),
        scratch=[pltpu.VMEM(x.shape, BF16) for x in sources[:3]]
        + [pltpu.SMEM(pattern.shape, jnp.int32)]
        + [pltpu.VMEM(x.shape, BF16) for x in sources[4:]]
        + [pltpu.SemaphoreType.DMA((len(sources),))],
        flops=PREPARE_FLOPS,
    )
    along_x = swap(along, "col", 1)
    solved_leaf, keep_a, send_a = call(
        leaf_a,
        [((leaves, size, width), BF16), ((early, size, half), F32), ((early, size, half), BF16)],
        leaf_inverse, leaf_rhs, leaf_lower, rhs,
        flops=2 * (1 + early) * leaves * size * size * width,
    )
    got_a = swap(send_a, "row", 1)
    pack_o = swap(pack, "row", 1)
    late = levels - early
    keep_b, send_b = call(
        leaf_b,
        [((late, size, half), F32), ((late, size, half), BF16)],
        solved_leaf, leaf_lower, rhs,
        flops=2 * late * leaves * size * size * width,
    )
    got_b = swap(send_b, "row", 1)
    sol0, kept1, sent1 = call(
        zero_a, [((size, half), BF16), kept, sent],
        keep_a, got_a, pack, pack_o, inverse_0,
        flops=4 * size * size * half,
    )
    got1 = swap(sent1, "col", 1)
    kept_m, got_m = {}, {}
    for m in range(early, levels):
        kept_m[m], sent_m = call(
            zero_next(m, m - early), [kept, sent], keep_b, got_b, sol0, pack, pack_o,
            flops=2 * size * size * half,
        )
        got_m[m] = swap(sent_m, "col", 1)
    along_xo = swap(along_x, "row", 1)
    side = swap(call(stack, [((4 * short, half), BF16)], along, along_x), "col", 2)
    sol1, sol1_for_x, u2, u3 = call(
        one, [((part_1, quarter), BF16)] * 2 + [kept] * 2,
        kept1, got1, inverse_1, pack, pack_o, along, along_x, along_xo,
        flops=6 * size * size * quarter,
    )
    w2 = call(difference, [sent], kept_m[2], got_m[2], u2)
    w2_y = swap(w2, "col", 2)
    sol0_o = swap(sol0, "row", 1)
    side_o = swap(side, "row", 1)
    s3 = call(difference, [sent], kept_m[3], got_m[3], u3)
    s3_y = swap(s3, "col", 2)
    sol1_x = swap(sol1_for_x, "col", 1)
    sol1_half = call(half_of, [((part_1, half), BF16)], sol1, sol1_x)
    sol1_o = swap(sol1_half, "row", 1)
    out1 = call(join, [((part_1, width), BF16)], sol1_half, sol1_o)
    out0 = call(join, [((size, width), BF16)], sol0, sol0_o)
    inv2, low2 = call(
        whole_2, [((size, size), BF16)] * 2,
        inverse_2, along, pack_o, along_x, along_xo, side, side_o, scratch=[pltpu.VMEM((size, size), F32)],
    )
    sol2, sol2_for_x, u3_2 = call(
        two, [((part_2, quarter), BF16)] * 2 + [kept], w2, w2_y, inv2, low2,
        flops=4 * size * size * quarter,
    )
    v3, to_x = call(top_share, [sent, ((part_3 + part_2, quarter), BF16)], s3, s3_y, u3_2, sol2_for_x, along_x)
    v3_xz = swap(v3, "col", 5)
    from_x = swap(to_x, "col", 1)
    v3_z = swap(v3, "col", 4)
    solved3 = call(
        three, [((part_3, half), F32)], v3, v3_z, v3_xz, inverse_3,
        scratch=[pltpu.VMEM((size, half), BF16)], flops=2 * inverse_3.size * half,
    )
    last = call(lay, [((part_2 + part_3, half), BF16)], solved3, from_x, sol2)
    last_o = swap(last, "row", 1)
    rest = call(join, [((part, width), BF16) for part in (part_2, part_3)], last, last_o)
    return (out0, out1, *rest)


def solution(mesh):
    return jax.shard_map(
        body,
        mesh=mesh,
        in_specs=(
            P(None, "col", "row", None),
            P(("col", "row"), None, None),
            P(("col", "row"), None, None),
            P(None, ("col", "row"), None, None),
            P("col", None),
            P("col", None),
            P("col", None),
            P("col", None),
            P(None, "row", "col"),
            P(None, "row", "col"),
            P(None, "row", "col"),
            P(None, "col", "row"),
        ),
        out_specs=(P("col", None), P("col", None), P("col", None), P("col", None)),
        check_vma=False,
    )
```
